768 devices in a mesh: gx: 96 (over z, x, core), gy: 8 (over y).
Axes of the slice: x: 4, y: 8, z: 12, core: 2. Of those that a mesh axis runs over, the one named last changes fastest.
Arguments:
- fields: float32 [4, 192, 8, 16, 8, 128], P(None, 'gx', None, 'gy'), may hold values from -6 to 6
- viscosity: float32 [192, 8, 16, 8, 128], P('gx', None, 'gy'), may hold values from 0.002 to 0.02
- inv_density: float32 [192, 16, 16], P('gx', 'gy'), may hold values from 0.5 to 2
- elem_group: int32 [192, 16, 16], P('gx', 'gy'), may hold values from 0 to 3
- coarse_inverse: float32 [3072, 3072], P(('gx', 'gy')), as said below
Outputs:
- fields_new: float32 [4, 192, 8, 16, 8, 128], P(None, 'gx', None, 'gy')
- pressure: float32 [192, 8, 16, 8, 128], P('gx', None, 'gy')
The draws below stay inside these ranges and needn't reach their ends.
Inputs may be any that keep to these rules, and one draw needn't show every extreme that they name: `elem_group`: the coarse unknown of an element among the 4 of its own device. `coarse_inverse`: symmetric and positive definite.
All inputs are finite; a program needn't handle non-finite values.
Results may differ from the reference program's by a relative error of at most 0.0015.
Values sent between devices are 32-bit elements; how exact they have to be, the bound alone decides.
A program may use at most 32 MiB of HBM per device.

```python
import math
import jax
import jax.numpy as jnp
import numpy as np
from jax import lax

ORDER = 7
EX = 2
EY = 2
EZ = 16
ITERS = 2
CHEB = 2
NCD = 4
NXE = 192
NYE = 16
NC = 3072
N_GX = 96
N_GY = 8


def draw_coarse_inverse(key, part):
    folded = jax.random.fold_in(key, 17)
    key_place, key_first, key_second, key_diag = jax.random.split(folded, 4)
    device = jnp.arange(NC, dtype=jnp.int32) // NCD
    half_x = max(N_GX // 2, 1)
    device_x = (device // N_GY % half_x).astype(jnp.float32)
    device_y = (device % N_GY).astype(jnp.float32)
    placed = jax.random.uniform(key_place, (NC, 2), jnp.float32, 0.0, 1.0)
    spot_x = device_x + placed[:, 0]
    spot_y = device_y + placed[:, 1]
    gap_x = spot_x[:, None] - spot_x[None, :]
    gap_y = spot_y[:, None] - spot_y[None, :]
    distance = jnp.sqrt(gap_x * gap_x + gap_y * gap_y)
    second = jnp.clip(jax.random.normal(key_second, (NC,), jnp.float32), -3.0, 3.0)
    reach = 3.0
    first = jnp.clip(jax.random.normal(key_first, (NC,), jnp.float32), -3.0, 3.0)
    diagonal = jax.random.uniform(key_diag, (NC,), jnp.float32, 1.0, 2.0)
    kernel = jnp.exp(-distance / reach)
    coupling = 0.2 * kernel * (first[:, None] * first[None, :] + second[:, None] * second[None, :])
    matrix = coupling + jnp.diag(diagonal)
    return (matrix / (1.0 * EX * EY * EZ)).astype(jnp.float32)


def plant(values, own_key, least, top_value):
    longest = values.shape.index(max(values.shape))
    spots = []
    for shift in (0, 1):
        where = [jax.random.randint(jax.random.fold_in(own_key, axis), (), 0, length) for axis, length in enumerate(values.shape)]
        where[longest] = (where[longest] + shift) % values.shape[longest]
        spots.append(tuple(where))
    return values.at[spots[0]].set(least).at[spots[1]].set(top_value)


def levels(rng, dims, shards, least, top_value):
    def one(position, parts):
        draws = jax.random.uniform(jax.random.fold_in(jax.random.fold_in(rng, 6), position), (parts,), jnp.float32, least / len(shards), top_value / len(shards))
        return jnp.repeat(jnp.exp(draws), dims[position] // parts).reshape((-1,) + (1,) * (len(dims) - position - 1))

    level = one(*shards[0])
    for cut in shards[1:]:
        level = level * one(*cut)
    return level


def normal_values(own_key, dims, width, bound, cuts=(), held_as=jnp.bfloat16):
    gain = levels(own_key, dims, cuts, -0.22, 0.18) if cuts else 1.0
    entries = jax.random.normal(own_key, dims, jnp.float32) * width * gain
    return jnp.minimum(jnp.maximum(entries, -bound), bound).astype(held_as)


def setup_inputs(seed: int = 0) -> dict:
    streams_of = jax.random.split(jax.random.key(seed), 6)
    return {
        "fields": normal_values(streams_of[0], (4, NXE, ORDER + 1, NYE, ORDER + 1, EZ * (ORDER + 1)), 1.0, 6.0, ((1, 96), (3, 8)), jnp.float32),
        "viscosity": jnp.clip(jnp.exp(math.log(0.02) - 2.30258502 * jax.random.uniform(streams_of[1], (NXE, ORDER + 1, NYE, ORDER + 1, EZ * (ORDER + 1)), jnp.float32) ** levels(streams_of[1], (NXE, ORDER + 1, NYE, ORDER + 1, EZ * (ORDER + 1)), ((0, 96), (2, 8)), -0.2, 0.2)), 0.002, 0.02),
        "inv_density": jnp.clip(jnp.exp(math.log(2.0) - 1.3862944 * jax.random.uniform(streams_of[2], (NXE, NYE, EZ), jnp.float32) ** levels(streams_of[2], (NXE, NYE, EZ), ((0, 96), (1, 8)), -0.2, 0.2)), 0.5, 2.0),
        "elem_group": plant(jax.random.randint(streams_of[3], (NXE, NYE, EZ), 0, NCD), jax.random.fold_in(streams_of[3], 1), 0, NCD - 1).astype(jnp.int32),
        "coarse_inverse": draw_coarse_inverse(jax.random.fold_in(streams_of[5], 71), 0),
    }


dt_step = 0.01
sigma_p = 4.0
prandtl = 0.7
cheb_ratio = 0.1


def tables():
    points = np.array([-1.0, -0.8717401485096066, -0.5917001814331423, -0.2092992179024789,
                       0.2092992179024789, 0.5917001814331423, 0.8717401485096066, 1.0])
    weights = np.array([1.0 / 28.0, 0.2107042271435061, 0.3411226924835044, 0.4124587946587038,
                        0.4124587946587038, 0.3411226924835044, 0.2107042271435061, 1.0 / 28.0])
    identity = np.eye(8)
    differ = points[:, None] - points[None, :] + identity
    barycentric = 1.0 / np.prod(differ, axis=1)
    offdiag = (barycentric[None, :] / barycentric[:, None]) / differ * (1.0 - identity)
    derivative = offdiag - identity * np.sum(offdiag, axis=1)[:, None]
    mass_one = identity * weights[None, :]
    stiff_one = derivative.T @ mass_one @ derivative
    stiff_three = (np.kron(np.kron(stiff_one, mass_one), mass_one)
                   + np.kron(np.kron(mass_one, stiff_one), mass_one)
                   + np.kron(np.kron(mass_one, mass_one), stiff_one))
    three_diag = np.sum(stiff_three * np.eye(512), axis=1)
    spectral_bound = float(np.max(np.sum(np.abs(stiff_three), axis=1) / three_diag))
    return derivative, weights, np.sum(stiff_one * identity, axis=1), spectral_bound


def join_pairs(field, elem_axis):
    node_axis = elem_axis + 1
    top_node = field.shape[node_axis] - 1
    last_face = lax.index_in_dim(field, top_node, node_axis, keepdims=False)
    first_face = lax.index_in_dim(field, 0, node_axis, keepdims=False)
    elem_count = field.shape[elem_axis]
    summed = (lax.slice_in_dim(last_face, 0, elem_count - 1, axis=elem_axis)
              + lax.slice_in_dim(first_face, 1, elem_count, axis=elem_axis))
    new_last = jnp.concatenate([summed, lax.slice_in_dim(last_face, elem_count - 1, elem_count, axis=elem_axis)], elem_axis)
    new_first = jnp.concatenate([lax.slice_in_dim(first_face, 0, 1, axis=elem_axis), summed], elem_axis)
    middle = lax.slice_in_dim(field, 1, top_node, axis=node_axis)
    return jnp.concatenate([jnp.expand_dims(new_first, node_axis), middle, jnp.expand_dims(new_last, node_axis)], node_axis)


def reference(fields, viscosity, inv_density, elem_group, coarse_inverse):
    precision = lax.Precision.HIGHEST
    derivative_np, weights_np, stiff_np, spectral_bound = tables()
    derivative = jnp.asarray(derivative_np, jnp.float32)
    weights_line = jnp.asarray(weights_np, jnp.float32)
    stiff_line = jnp.asarray(stiff_np, jnp.float32)
    line_nodes = ORDER + 1
    elems_x = fields.shape[1]
    elems_y = fields.shape[3]
    length = fields.shape[5]
    elems_z = length // line_nodes

    def split_z(field):
        return field.reshape(field.shape[:-1] + (elems_z, line_nodes))

    def merge_z(field):
        return field.reshape(field.shape[:-2] + (length,))

    def gradient(field):
        along_x = jnp.einsum('ia,cxaybl->cxiybl', derivative, field, precision=precision)
        along_y = jnp.einsum('jb,cxaybl->cxayjl', derivative, field, precision=precision)
        along_z = merge_z(jnp.einsum('kq,cxaybzq->cxaybzk', derivative, split_z(field), precision=precision))
        return along_x, along_y, along_z

    def adjoint(first_part, second_part, third_part):
        result = jnp.einsum('ai,cxaybl->cxiybl', derivative, first_part, precision=precision)
        result = result + jnp.einsum('bj,cxaybl->cxayjl', derivative, second_part, precision=precision)
        return result + merge_z(jnp.einsum('qk,cxaybzq->cxaybzk', derivative, split_z(third_part), precision=precision))

    def assemble(field):
        field = join_pairs(field, 1)
        field = join_pairs(field, 3)
        return merge_z(join_pairs(split_z(field), 5))

    def on_x(values):
        return values[None, :, None, None, None]

    def on_y(values):
        return values[None, None, None, :, None]

    weights_z = jnp.tile(weights_line, elems_z)
    stiff_z = jnp.tile(stiff_line, elems_z)
    weight = on_x(weights_line) * on_y(weights_line) * weights_z
    diag_stiff = (on_x(stiff_line) * on_y(weights_line) * weights_z
                  + on_x(weights_line) * on_y(stiff_line) * weights_z
                  + on_x(weights_line) * on_y(weights_line) * stiff_z)
    kappa = jnp.repeat(inv_density, line_nodes, axis=2)[:, None, :, None, :]
    unit = jnp.ones((1, elems_x, line_nodes, elems_y, line_nodes, length), jnp.float32)
    multiplicity = assemble(unit)[0]
    mass_sum = assemble(unit * weight)[0]
    pdiag = assemble((kappa * diag_stiff + sigma_p * weight)[None])[0]
    start = assemble(fields * weight) / mass_sum
    velocity = start[:3]
    factors = [1.0, 1.0, 1.0, 1.0 / prandtl]
    updated = []
    for channel in range(4):
        field = start[channel:channel + 1]
        along_x, along_y, along_z = gradient(field)
        advect = velocity[0] * along_x + velocity[1] * along_y + velocity[2] * along_z
        scaled = factors[channel] * viscosity * weight
        rhs = -weight * advect - adjoint(scaled * along_x, scaled * along_y, scaled * along_z)
        updated.append(field + dt_step * assemble(rhs) / mass_sum)
    fields_new = jnp.concatenate(updated, 0)

    div_x = jnp.einsum('ia,xaybl->xiybl', derivative, fields_new[0], precision=precision)
    div_y = jnp.einsum('jb,xaybl->xayjl', derivative, fields_new[1], precision=precision)
    div_z = merge_z(jnp.einsum('kq,xaybzq->xaybzk', derivative, split_z(fields_new[2]), precision=precision))
    rhs_p = assemble((-weight * (div_x + div_y + div_z))[None])[0]

    inv_mult = 1.0 / multiplicity
    inv_diag = 1.0 / pdiag
    kappa_weight = kappa * weight

    def apply_op(field):
        along_x, along_y, along_z = gradient(field[None])
        local = adjoint(kappa_weight * along_x, kappa_weight * along_y, kappa_weight * along_z)[0] + sigma_p * weight * field
        return assemble(local[None])[0]

    def inner_product(first_field, second_field):
        return jnp.sum(first_field * second_field * inv_mult)

    device_x = jnp.arange(elems_x, dtype=jnp.int32) // EX
    device_y = jnp.arange(elems_y, dtype=jnp.int32) // EY
    coarse_ids = NCD * (device_x[:, None, None] * N_GY + device_y[None, :, None]) + elem_group

    def restrict(resid):
        elem_sums = split_z(resid * inv_mult).sum(axis=(1, 3, 5))
        return jax.ops.segment_sum(elem_sums.reshape(-1), coarse_ids.reshape(-1), num_segments=NC)

    def prolong(values):
        elem_values = values[coarse_ids]
        local = jnp.repeat(elem_values, line_nodes, axis=2)[:, None, :, None, :] * inv_mult
        return assemble(local[None])[0]

    upper = spectral_bound
    lower = cheb_ratio * upper
    cheb_theta = 0.5 * (upper + lower)
    cheb_delta = 0.5 * (upper - lower)

    def precondition(resid):
        update = resid * inv_diag / cheb_theta
        smoothed = update
        cheb_rho = cheb_delta / cheb_theta
        for step in range(CHEB - 1):
            defect = resid - apply_op(smoothed)
            rho_next = 1.0 / (2.0 * cheb_theta / cheb_delta - cheb_rho)
            update = rho_next * cheb_rho * update + (2.0 * rho_next / cheb_delta) * defect * inv_diag
            smoothed = smoothed + update
            cheb_rho = rho_next
        coarse_values = jnp.dot(coarse_inverse, restrict(resid), precision=precision)
        return smoothed + prolong(coarse_values)

    pressure = jnp.zeros_like(rhs_p)
    resid = rhs_p
    precond_r = precondition(resid)
    rz_value = inner_product(resid, precond_r)
    direction = precond_r
    for iteration in range(ITERS):
        image = apply_op(direction)
        step_size = rz_value / inner_product(direction, image)
        pressure = pressure + step_size * direction
        if iteration + 1 < ITERS:
            resid = resid - step_size * image
            precond_r = precondition(resid)
            rz_next = inner_product(resid, precond_r)
            direction = precond_r + (rz_next / rz_value) * direction
            rz_value = rz_next
    return fields_new, pressure
```

```python
import functools

import jax
import jax.numpy as jnp
import numpy as np
from jax import lax
from jax.experimental import pallas as pl
from jax.experimental.pallas import tpu as pltpu
from jax.sharding import PartitionSpec as P

NCD = 4
XC = 8
YL = 8

dt_step = 0.01
sigma_p = 4.0
prandtl = 0.7
cheb_ratio = 0.1

F32 = jnp.float32
BF16 = jnp.bfloat16
DIRS = [(-1, 0), (1, 0), (0, -1), (0, 1), (-1, -1), (-1, 1), (1, -1), (1, 1)]
MESH = pl.DeviceIdType.MESH


def tables():
    points = np.array(
        [
            -1.0,
            -0.8717401485096066,
            -0.5917001814331423,
            -0.2092992179024789,
            0.2092992179024789,
            0.5917001814331423,
            0.8717401485096066,
            1.0,
        ]
    )
    weights = np.array(
        [
            1.0 / 28.0,
            0.2107042271435061,
            0.3411226924835044,
            0.4124587946587038,
            0.4124587946587038,
            0.3411226924835044,
            0.2107042271435061,
            1.0 / 28.0,
        ]
    )
    identity = np.eye(8)
    differ = points[:, None] - points[None, :] + identity
    barycentric = 1.0 / np.prod(differ, axis=1)
    offdiag = barycentric[None, :] / barycentric[:, None] / differ * (1.0 - identity)
    derivative = offdiag - identity * np.sum(offdiag, axis=1)[:, None]
    mass_one = identity * weights[None, :]
    stiff_one = derivative.T @ mass_one @ derivative
    stiff_three = (
        np.kron(np.kron(stiff_one, mass_one), mass_one)
        + np.kron(np.kron(mass_one, stiff_one), mass_one)
        + np.kron(np.kron(mass_one, mass_one), stiff_one)
    )
    three_diag = np.sum(stiff_three * np.eye(512), axis=1)
    spectral_bound = float(np.max(np.sum(np.abs(stiff_three), axis=1) / three_diag))
    return derivative, weights, stiff_one, spectral_bound


DER, WTS, STF, SBOUND = tables()
KLN = np.diag(STF)


def constants():
    cols = np.stack([DER, DER.T, STF], 0)
    cy = np.broadcast_to(np.transpose(cols, (0, 2, 1))[:, :, :, None], (3, 8, 8, 128))

    def big(one):
        full = np.kron(np.eye(16), one).astype(np.float32)
        high = np.asarray(full, dtype=jnp.bfloat16)
        low = np.asarray(full - high.astype(np.float32), dtype=jnp.bfloat16)
        return np.block([[high, low], [high, np.zeros_like(low)]])

    bz = np.stack([big(DER.T), big(DER), big(STF)], 0)
    wy = np.tile(WTS, 2)[:, None]
    ky = np.tile(KLN, 2)[:, None]
    wz = np.tile(WTS, 16)[None, :]
    kz = np.tile(KLN, 16)[None, :]
    one = np.ones((16, 128))
    cp = np.stack([wy * wz, one * wz, wy * one, ky * wz + wy * kz, 1.0 / (wy * wz)], 0)
    spread = np.kron(np.eye(16), np.ones((1, 8)))
    return (
        jnp.asarray(np.ascontiguousarray(cy), F32),
        jnp.asarray(bz, BF16),
        jnp.asarray(cp, F32),
        jnp.asarray(spread, F32),
    )


def kernel(
    nx, ny, nxc,
    fields, visc, dens, grp, coarse, cy, bz, cp, spr,
    out_f, out_p,
    F, FN, V, L4, L1, W, IM, KAP, INVD, CX, AUX, AUXR, OH, PC,
    T1, T2, T3, R0, S0, Z0, W1, ZI,
    sx4, sy4, sc4, rx4, ry4, rc4, sx1, sy1, sc1, rx1, ry1, rc1,
    ag1, ag2, ag3,
    s_sem, r_sem, as_sem, ar_sem, cs_sem, cr_sem, gs_sem, gr_sem, l_sem,
):
    gx = lax.axis_index("gx")
    gy = lax.axis_index("gy")
    nz = nx // nxc
    xc = gx % nxc
    zc = gx // nxc

    def nbr(dx, dy):
        return ((gx + dx + nx) % nx, (gy + dy + ny) % ny)

    def y_mate(k):
        return (gx, (gy + k) % ny)

    def x_mate(k):
        return (zc * nxc + (xc + k) % nxc, gy)

    def z_mate(k):
        return (((zc + k) % nz) * nxc + xc, gy)

    mates = [nbr(dx, dy) for dx, dy in DIRS]
    mates += [y_mate(k) for k in range(1, ny)]
    mates += [x_mate(k) for k in range(1, nxc)]
    mates += [z_mate(k) for k in range(1, nz)]
    barrier = pltpu.get_barrier_semaphore()
    for mate in mates:
        pl.semaphore_signal(barrier, inc=1, device_id=mate, device_id_type=MESH)

    load_f = pltpu.make_async_copy(fields, F, l_sem.at[0])
    load_v = pltpu.make_async_copy(visc, V, l_sem.at[1])
    load_c = pltpu.make_async_copy(coarse, CX.at[8], l_sem.at[2])
    load_f.start()
    load_v.start()
    load_c.start()

    lane = lax.broadcasted_iota(jnp.int32, (8, 128), 1)
    sub = lax.broadcasted_iota(jnp.int32, (8, 128), 0)
    one = jnp.float32(1.0)
    zero = jnp.float32(0.0)
    j7 = jnp.where((lane % 8 == 7) & (lane < 127), one, zero)
    j0 = jnp.where((lane % 8 == 0) & (lane > 0), one, zero)
    j7p = jnp.concatenate([j7, j7], 0)
    j0p = jnp.concatenate([j0, j0], 0)
    s0 = jnp.where(sub == 0, one, zero)
    s7 = jnp.where(sub == 7, one, zero)

    has_l = jnp.where(gx > 0, one, zero)
    has_r = jnp.where(gx < nx - 1, one, zero)
    has_b = jnp.where(gy > 0, one, zero)
    has_t = jnp.where(gy < ny - 1, one, zero)
    vx = {-1: has_l, 0: one, 1: has_r}
    vy = {-1: has_b, 0: one, 1: has_t}

    def zjoin(v):
        return v + j7p * pltpu.roll(v, 127, 1) + j0p * pltpu.roll(v, 1, 1)

    def rows(x, base=0):
        return pl.ds(base + 16 * x, 16)

    def xyjoin(L, base=0):
        both = L[pl.ds(base + 112, 16), :] + L[pl.ds(base + 128, 16), :]
        L[pl.ds(base + 112, 16), :] = both
        L[pl.ds(base + 128, 16), :] = both
        pair = L[pl.ds(base + 7, 16, stride=16), :] + L[pl.ds(base + 8, 16, stride=16), :]
        L[pl.ds(base + 7, 16, stride=16), :] = pair
        L[pl.ds(base + 8, 16, stride=16), :] = pair

    def yop(plane, which):
        parts = []
        for t in range(2):
            tile = plane[8 * t : 8 * t + 8, :]
            total = None
            for b in range(8):
                term = jnp.broadcast_to(tile[b : b + 1, :], (8, 128)) * cy[which, b]
                total = term if total is None else total + term
            parts.append(total)
        return jnp.concatenate(parts, 0)

    def xop(planes, coef):
        total = None
        for a in range(8):
            term = planes[a] * jnp.float32(coef[a])
            total = term if total is None else total + term
        return total

    def zop(f, which):
        high = f.astype(BF16)
        low = (f - high.astype(F32)).astype(BF16)
        both = jnp.concatenate([high, low], 1)
        prod = jnp.dot(both, bz[which], preferred_element_type=F32)
        return prod[:, :128] + prod[:, 128:]

    def faces(L, nch, e, sx, sy, sc, rx, ry, rc, num):
        for c in range(nch):
            base = 256 * c
            sx[e, 0, pl.ds(16 * c, 16), :] = L[pl.ds(base, 16), :]
            sx[e, 1, pl.ds(16 * c, 16), :] = L[pl.ds(base + 240, 16), :]
            sy[e, 0, pl.ds(16 * c, 16), :] = L[pl.ds(base, 16, stride=16), :]
            sy[e, 1, pl.ds(16 * c, 16), :] = L[pl.ds(base + 15, 16, stride=16), :]
            for k, (dx, dy) in enumerate(DIRS[4:]):
                row = base + (240 if dx > 0 else 0) + (15 if dy > 0 else 0)
                sc[e, k, pl.ds(c, 1), :] = L[pl.ds(row, 1), :]
        copies = []
        for d in (4, 5, 6, 7, 0, 1, 2, 3):
            if d < 2:
                src, dst = sx.at[e, d], rx.at[e, d]
            elif d < 4:
                src, dst = sy.at[e, d - 2], ry.at[e, d - 2]
            else:
                src, dst = sc.at[e, d - 4], rc.at[e, d - 4]
            copy = pltpu.make_async_remote_copy(
                src, dst, s_sem.at[num, d], r_sem.at[num, d],
                device_id=nbr(*DIRS[d]), device_id_type=MESH,
            )
            copy.start()
            copies.append(copy)
        return copies

    def finish(copies, L, nch, e, rx, ry, rc):
        for copy in copies:
            copy.wait_recv()
        for c in range(nch):
            base = 256 * c
            at = pl.ds(16 * c, 16)
            lo, hi = pl.ds(base, 16), pl.ds(base + 240, 16)
            L[lo, :] = L[lo, :] + has_l * rx[e, 1, at, :]
            L[hi, :] = L[hi, :] + has_r * rx[e, 0, at, :]
            lo, hi = pl.ds(base, 16, stride=16), pl.ds(base + 15, 16, stride=16)
            L[lo, :] = L[lo, :] + has_b * ry[e, 1, at, :]
            L[hi, :] = L[hi, :] + has_t * ry[e, 0, at, :]
            for k, (dx, dy) in enumerate(DIRS[4:]):
                row = pl.ds(base + (0 if dx > 0 else 240) + (0 if dy > 0 else 15), 1)
                L[row, :] = L[row, :] + (vx[-dx] * vy[-dy]) * rc[e, k, pl.ds(c, 1), :]

    set4 = (sx4, sy4, sc4, rx4, ry4, rc4)
    set1 = (sx1, sy1, sc1, rx1, ry1, rc1)
    pending = []

    for ex in range(2):
        AUX[pl.ds(2 * ex, 2), :] = jnp.dot(
            dens[ex], spr[...], preferred_element_type=F32, precision=lax.Precision.HIGHEST
        )
        AUX[pl.ds(4 + 2 * ex, 2), :] = jnp.dot(
            grp[ex].astype(F32), spr[...], preferred_element_type=F32,
            precision=lax.Precision.HIGHEST,
        )
    for ex in range(2):
        for ey in range(2):
            row = AUX[pl.ds(2 * ex + ey, 1), :]
            KAP[pl.ds(16 * ex + 8 * ey, 8), :] = jnp.broadcast_to(row, (8, 128))

    half = jnp.float32(0.5)
    imx = [one] * 16
    imx[0] = jnp.where(gx > 0, half, one)
    imx[7] = imx[8] = half
    imx[15] = jnp.where(gx < nx - 1, half, one)
    imz = one - half * (j7 + j0)
    imy0 = one - half * s7 - (half * has_b) * s0
    imy1 = one - half * s0 - (half * has_t) * s7
    imyz = jnp.concatenate([imy0 * imz, imy1 * imz], 0)
    for x in range(16):
        W[rows(x), :] = jnp.float32(WTS[x % 8]) * cp[0]
        IM[rows(x), :] = imx[x] * imyz

    load_f.wait()
    for c in range(4):
        for x in range(16):
            L4[rows(x, 256 * c), :] = zjoin(F[rows(x, 256 * c), :])
        xyjoin(L4, 256 * c)
    pl.semaphore_wait(barrier, len(mates))
    now = faces(L4, 4, 0, *set4, 0)
    pending += now
    side = []
    for d, (dx, dy) in enumerate(DIRS):
        copy = pltpu.make_async_remote_copy(
            AUX, AUXR.at[d], as_sem.at[d], ar_sem.at[d],
            device_id=nbr(dx, dy), device_id_type=MESH,
        )
        copy.start()
        side.append(copy)
    load_c.wait()
    rowsc = []
    for d, (dx, dy) in enumerate(DIRS):
        copy = pltpu.make_async_remote_copy(
            CX.at[8], CX.at[d], cs_sem.at[d], cr_sem.at[d],
            device_id=nbr(dx, dy), device_id_type=MESH,
        )
        copy.start()
        rowsc.append(copy)
    load_v.wait()
    V[...] = V[...] * W[...]
    finish(now, L4, 4, 0, rx4, ry4, rc4)
    for c in range(4):
        at = pl.ds(256 * c, 256)
        F[at, :] = L4[at, :] * IM[...]

    def channel(c, carry):
        base = pl.multiple_of(c * 256, 256)
        coef = jnp.where(c == 3, jnp.float32(1.0 / prandtl), one)
        T3[...] = zop(F[pl.ds(base, 256), :], 0)
        for ex in range(2):
            planes = [F[pl.ds(base + 16 * (8 * ex + a), 16), :] for a in range(8)]
            for i in range(8):
                x = 8 * ex + i
                gxp = xop(planes, DER[i])
                gyp = yop(planes[i], 0)
                gzp = T3[rows(x), :]
                adv = (
                    F[rows(x), :] * gxp + F[rows(x, 256), :] * gyp + F[rows(x, 512), :] * gzp
                )
                nuw = coef * V[rows(x), :]
                T1[rows(x), :] = nuw * gxp
                T2[rows(x), :] = yop(nuw * gyp, 1) + W[rows(x), :] * adv
                T3[rows(x), :] = nuw * gzp
        T3[...] = zop(T3[...], 1) + T2[...]
        for ex in range(2):
            planes = [T1[rows(8 * ex + a), :] for a in range(8)]
            for i in range(8):
                x = 8 * ex + i
                total = xop(planes, DER[:, i]) + T3[rows(x), :]
                L4[pl.ds(base + 16 * x, 16), :] = zjoin(-total)
        xyjoin(L4, base)
        return carry

    lax.fori_loop(0, 4, channel, 0)
    now = faces(L4, 4, 1, *set4, 1)
    pending += now

    for copy in side:
        copy.wait_recv()

    def where_from(ex, ey):
        dx = -1 if ex == 0 else (1 if ex == 3 else 0)
        dy = -1 if ey == 0 else (1 if ey == 3 else 0)
        lx = {0: 1, 1: 0, 2: 1, 3: 0}[ex]
        ly = {0: 1, 1: 0, 2: 1, 3: 0}[ey]
        return dx, dy, 2 * lx + ly

    def slot_of(dx, dy):
        return 8 if (dx, dy) == (0, 0) else DIRS.index((-dx, -dy))

    kgrid = []
    for ex in range(4):
        line = []
        for ey in range(4):
            dx, dy, local = where_from(ex, ey)
            slot = slot_of(dx, dy)
            valid = vx[dx] * vy[dy]
            if slot == 8:
                krow = AUX[pl.ds(local, 1), :]
                grow = AUX[pl.ds(4 + local, 1), :]
            else:
                krow = AUXR[slot, pl.ds(local, 1), :]
                grow = AUXR[slot, pl.ds(4 + local, 1), :]
            line.append(krow * valid)
            hit = jnp.abs(jnp.broadcast_to(grow, (4, 128)) - sub[0:4].astype(F32)) < half
            OH[4 * ex + ey] = jnp.where(hit, valid, zero)
        kgrid.append(line)

    xsets = [(0, 1), (1,), (1, 2), (2,), (2, 3)]
    xclass = [0] + [1] * 6 + [2, 2] + [3] * 6 + [4]

    def spread(grid):
        planes = []
        for members in xsets:
            e = []
            for ey in range(4):
                total = grid[members[0]][ey]
                for ex in members[1:]:
                    total = total + grid[ex][ey]
                e.append(jnp.broadcast_to(total, (8, 128)))
            low = e[1] + s0 * e[0] + s7 * e[2]
            high = e[2] + s0 * e[1] + s7 * e[3]
            planes.append(zjoin(jnp.concatenate([low, high], 0)))
        return planes

    kplanes = spread(kgrid)
    mult = one / imyz
    for x in range(16):
        wa = jnp.float32(WTS[x % 8])
        ka = jnp.float32(KLN[x % 8])
        diag = (ka * cp[0] + wa * cp[3]) * kplanes[xclass[x]] + (
            jnp.float32(sigma_p) * wa / imx[x]
        ) * cp[0] * mult
        INVD[rows(x), :] = one / diag

    group = lane // 32

    def ag_start(a, row):
        ag1[a, 0] = row
        out = []
        for k in range(1, ny):
            copy = pltpu.make_async_remote_copy(
                ag1.at[a, 0], ag1.at[a, k], gs_sem.at[a, 0, k], gr_sem.at[a, 0, k],
                device_id=y_mate(k), device_id_type=MESH,
            )
            copy.start()
            out.append(copy)
        return out

    def ag_second(a, copies):
        for copy in copies:
            copy.wait_recv()
        row = ag1[a, 0]
        for k in range(1, ny):
            row = row + ag1[a, k]
        wide = jnp.broadcast_to(row, (8, 128))
        message = jnp.zeros((8, 128), F32)
        for s in range(4):
            turned = wide if s == 0 else pltpu.roll(wide, 32 * s, 1)
            for g in range(4):
                to = (g + s) % 4
                if g == 3:
                    row_at, to_at = 2, 1
                else:
                    t = xc + (g - 1)
                    low = t < 0
                    high = t > XC - 1
                    row_at = jnp.where(low | high, 2, t // 4)
                    to_at = jnp.where(low, 3, jnp.where(high, 0, t % 4))
                take = (sub == row_at) & (group == to_at) & (group == to)
                message = message + jnp.where(take, turned, zero)
        ag2[a, 0] = message[0:4]
        out = []
        for k in range(1, nxc):
            copy = pltpu.make_async_remote_copy(
                ag2.at[a, 0], ag2.at[a, k], gs_sem.at[a, 1, k], gr_sem.at[a, 1, k],
                device_id=x_mate(k), device_id_type=MESH,
            )
            copy.start()
            out.append(copy)
        return out

    def ag_third(a, copies):
        for copy in copies:
            copy.wait_recv()
        message = ag2[a, 0]
        for k in range(1, nxc):
            message = message + ag2[a, k]
        ag3[a, zc] = message
        out = []
        for k in range(1, nz):
            copy = pltpu.make_async_remote_copy(
                ag3.at[a, zc], ag3.at[a, zc], gs_sem.at[a, 2, k], gr_sem.at[a, 2, k],
                device_id=z_mate(k), device_id_type=MESH,
            )
            copy.start()
            out.append(copy)
        return out

    def ag_end(a, copies):
        for copy in copies:
            copy.wait_recv()

    def sums(a, count):
        total = ag3[a, 0][2:3]
        for z in range(1, nz):
            total = total + ag3[a, z][2:3]
        lanes = lane[0:1]
        return [
            jnp.sum(jnp.where(lanes == 32 + k, total, zero), axis=1, keepdims=True)
            for k in range(count)
        ]

    devs = [(dx, dy) for dx in (-1, 0, 1) for dy in (-1, 0, 1)]
    members = {dev: [] for dev in devs}
    for ex in range(4):
        for ey in range(4):
            dx, dy, _ = where_from(ex, ey)
            members[(dx, dy)].append((ex, ey))

    def restricted(L):
        x_first = imx[0] * L[rows(0), :]
        x_last = imx[15] * L[rows(15), :]
        low, high = x_first, x_last
        for x in range(1, 7):
            low = low + L[rows(x), :]
            high = high + L[rows(x + 8), :]
        low = low + half * L[rows(7), :]
        high = high + half * L[rows(8), :]
        grid = []
        for part in (x_first, low, high, x_last):
            part = part * imyz
            t0, t1 = part[0:8], part[8:16]
            grid.append(
                [
                    t0[0:1],
                    jnp.sum(t0, axis=0, keepdims=True),
                    jnp.sum(t1, axis=0, keepdims=True),
                    t1[7:8],
                ]
            )
        message = jnp.zeros((4, 128), F32)
        for dx, dy in devs:
            acc = None
            for ex, ey in members[(dx, dy)]:
                term = jnp.broadcast_to(grid[ex][ey], (4, 128)) * OH[4 * ex + ey]
                acc = term if acc is None else acc + term
            value = jnp.sum(acc, axis=1, keepdims=True)
            to = 32 * (dx + 1) + ((gy + dy + YL) % YL) * NCD + sub[0:4]
            message = message + jnp.where(lane[0:4] == to, value, zero)
        return jnp.sum(message, axis=0, keepdims=True)

    def with_sums(row, values):
        lanes = lane[0:1]
        for k, value in enumerate(values):
            row = row + jnp.where(lanes == 96 + k, value, zero)
        return row

    def coarse_planes(a):
        lanes = lane[0:1]
        accs = [None] * 9
        for z in range(nz):
            own = ag3[a, z]
            first, second = own[0:1], own[1:2]
            if z > 0:
                first = first + jnp.where(lanes < 32, ag3[a, z - 1][2:3], zero)
            if z < nz - 1:
                second = second + jnp.where(lanes >= 96, ag3[a, z + 1][2:3], zero)
            for h, part in enumerate((first, second)):
                wide = jnp.broadcast_to(part, (4, 128))
                for n in range(9):
                    term = CX[n, :, pl.ds((2 * z + h) * 128, 128)] * wide
                    accs[n] = term if accs[n] is None else accs[n] + term
        values = [jnp.sum(acc, axis=1, keepdims=True) for acc in accs]
        grid = []
        for ex in range(4):
            line = []
            for ey in range(4):
                dx, dy, _ = where_from(ex, ey)
                value = values[slot_of(dx, dy)]
                line.append(jnp.sum(OH[4 * ex + ey] * value, axis=0, keepdims=True))
            grid.append(line)
        return [plane * imyz for plane in spread(grid)]

    def apply_local(q, put):
        T3[...] = zop(q[...], 2)
        for ex in range(2):
            planes = [q[rows(8 * ex + a), :] for a in range(8)]
            kap = KAP[pl.ds(16 * ex, 16), :]
            for i in range(8):
                x = 8 * ex + i
                wa = jnp.float32(WTS[i])
                kx = xop(planes, STF[i])
                ky = yop(planes[i], 2)
                inner = cp[0] * kx + wa * (cp[1] * ky + cp[2] * T3[rows(x), :])
                put(x, planes[i], kap * inner + (jnp.float32(sigma_p) * wa) * (cp[0] * planes[i]))

    def put_joined(x, plane, value):
        L1[rows(x), :] = zjoin(value)

    upper = SBOUND
    lower = cheb_ratio * upper
    theta = 0.5 * (upper + lower)
    delta = 0.5 * (upper - lower)
    rho = delta / theta
    rho_next = 1.0 / (2.0 * theta / delta - rho)
    c2 = 2.0 * rho_next / delta
    c1 = jnp.float32((1.0 + rho_next * rho) / theta + c2)
    c2 = jnp.float32(c2 / theta)

    finish(now, L4, 4, 1, rx4, ry4, rc4)
    for x in range(16):
        scale = (jnp.float32(dt_step / WTS[x % 8]) * imx[x]) * (imyz * cp[4])
        for c in range(4):
            at = rows(x, 256 * c)
            FN[at, :] = F[at, :] + L4[at, :] * scale
    store_f = pltpu.make_async_copy(FN, out_f, l_sem.at[3])
    store_f.start()
    T3[...] = zop(FN[pl.ds(512, 256), :], 0)
    for ex in range(2):
        planes = [FN[rows(8 * ex + a), :] for a in range(8)]
        for i in range(8):
            x = 8 * ex + i
            div = xop(planes, DER[i]) + yop(FN[rows(x, 256), :], 0) + T3[rows(x), :]
            L1[rows(x), :] = zjoin(-(W[rows(x), :] * div))
    xyjoin(L1)

    ga = ag_start(0, restricted(L1))
    now = faces(L1, 1, 0, *set1, 2)
    pending += now
    pend_g = list(ga)
    finish(now, L1, 1, 0, rx1, ry1, rc1)
    R0[...] = L1[...]
    T1[...] = L1[...] * INVD[...]
    apply_local(T1, put_joined)
    xyjoin(L1)
    now = faces(L1, 1, 1, *set1, 3)
    pending += now
    ga = ag_second(0, ga)
    pend_g += ga
    ga = ag_third(0, ga)
    pend_g += ga
    finish(now, L1, 1, 1, rx1, ry1, rc1)
    S0[...] = c1 * T1[...] - c2 * (INVD[...] * L1[...])
    for copy in rowsc:
        copy.wait_recv()
    ag_end(0, ga)
    planes = coarse_planes(0)
    for x in range(16):
        Z0[rows(x), :] = S0[rows(x), :] + imx[x] * planes[xclass[x]]

    dot = []

    def put_first(x, plane, value):
        W1[rows(x), :] = value
        L1[rows(x), :] = zjoin(value)
        term = plane * value
        dot.append(term if not dot else dot.pop() + term)

    def full(v):
        return jnp.sum(jnp.sum(v, axis=0, keepdims=True), axis=1, keepdims=True)

    apply_local(Z0, put_first)
    xyjoin(L1)
    rz_part = None
    for x in range(16):
        term = imx[x] * (R0[rows(x), :] * Z0[rows(x), :])
        rz_part = term if rz_part is None else rz_part + term
    row = with_sums(restricted(L1), [full(rz_part * imyz), full(dot.pop())])
    ga = ag_start(1, row)
    pend_g += ga
    now = faces(L1, 1, 2, *set1, 4)
    pending += now
    finish(now, L1, 1, 2, rx1, ry1, rc1)
    T2[...] = L1[...]
    T1[...] = L1[...] * INVD[...]
    apply_local(T1, put_joined)
    xyjoin(L1)
    now = faces(L1, 1, 3, *set1, 5)
    pending += now
    ga = ag_second(1, ga)
    pend_g += ga
    ga = ag_third(1, ga)
    pend_g += ga
    finish(now, L1, 1, 3, rx1, ry1, rc1)
    ZI[...] = c1 * T1[...] - c2 * (INVD[...] * L1[...])
    ag_end(1, ga)
    rz0, curv0 = sums(1, 2)
    step0 = rz0 / curv0
    planes = coarse_planes(1)
    rz_part = None
    for x in range(16):
        at = rows(x)
        zi = ZI[at, :] + imx[x] * planes[xclass[x]]
        z1 = Z0[at, :] - step0 * zi
        ZI[at, :] = z1
        term = imx[x] * ((R0[at, :] - step0 * T2[at, :]) * z1)
        rz_part = term if rz_part is None else rz_part + term

    dots = [None, None]

    def put_second(x, plane, value):
        terms = (plane * value, Z0[rows(x), :] * value + plane * W1[rows(x), :])
        for k in range(2):
            dots[k] = terms[k] if dots[k] is None else dots[k] + terms[k]

    apply_local(ZI, put_second)
    row = with_sums(
        jnp.zeros((1, 128), F32), [full(rz_part * imyz), full(dots[0]), full(dots[1])]
    )
    ga = ag_start(2, row)
    pend_g += ga
    ga = ag_second(2, ga)
    pend_g += ga
    ga = ag_third(2, ga)
    pend_g += ga
    ag_end(2, ga)
    rz1, a11, a10 = sums(2, 3)
    beta = rz1 / rz0
    curv1 = a11 + beta * a10 + beta * beta * curv0
    step1 = rz1 / curv1
    PC[...] = (step0 + step1 * beta) * Z0[...] + step1 * ZI[...]
    store_p = pltpu.make_async_copy(PC, out_p, l_sem.at[4])
    store_p.start()

    for copy in pending + side + rowsc + pend_g:
        copy.wait_send()
    store_f.wait()
    store_p.wait()


def per_device(nx, ny, nxc, fields, viscosity, inv_density, elem_group, coarse_inverse):
    nz = nx // nxc
    cy, bz, cp, spr = constants()
    coarse = coarse_inverse
    if nxc * ny != XC * YL:
        coarse = coarse.reshape(NCD, nz, nxc, ny, NCD)
        coarse = jnp.pad(coarse, ((0, 0), (0, 0), (0, XC - nxc), (0, YL - ny), (0, 0)))
        coarse = coarse.reshape(NCD, nz * XC * YL * NCD)
    ncp = coarse.shape[1]

    def vm(*shape):
        return pltpu.VMEM(shape, F32)

    field = vm(256, 128)
    scratch = [
        vm(1024, 128), vm(1024, 128), field, vm(1024, 128), field, field, field,
        vm(32, 128), field, vm(9, NCD, ncp), vm(8, 128), vm(8, 8, 128), vm(16, 4, 128), field,
        field, field, field, field, field, field, field, field,
        vm(2, 2, 64, 128), vm(2, 2, 64, 128), vm(2, 4, 4, 128),
        vm(2, 2, 64, 128), vm(2, 2, 64, 128), vm(2, 4, 4, 128),
        vm(4, 2, 16, 128), vm(4, 2, 16, 128), vm(4, 4, 1, 128),
        vm(4, 2, 16, 128), vm(4, 2, 16, 128), vm(4, 4, 1, 128),
        vm(3, ny, 1, 128), vm(3, nxc, 4, 128), vm(3, nz, 4, 128),
        pltpu.SemaphoreType.DMA((6, 8)), pltpu.SemaphoreType.DMA((6, 8)),
        pltpu.SemaphoreType.DMA((8,)), pltpu.SemaphoreType.DMA((8,)),
        pltpu.SemaphoreType.DMA((8,)), pltpu.SemaphoreType.DMA((8,)),
        pltpu.SemaphoreType.DMA((3, 3, 12)), pltpu.SemaphoreType.DMA((3, 3, 12)),
        pltpu.SemaphoreType.DMA((5,)),
    ]
    anywhere = pl.BlockSpec(memory_space=pl.ANY)
    inside = pl.BlockSpec(memory_space=pltpu.VMEM)
    new, pressure = pl.pallas_call(
        functools.partial(kernel, nx, ny, nxc),
        out_shape=(
            jax.ShapeDtypeStruct((1024, 128), F32),
            jax.ShapeDtypeStruct((256, 128), F32),
        ),
        in_specs=[anywhere, anywhere, inside, inside, anywhere, inside, inside, inside, inside],
        out_specs=(anywhere, anywhere),
        scratch_shapes=scratch,
        compiler_params=pltpu.CompilerParams(collective_id=0, has_side_effects=True),
    )(
        fields.reshape(1024, 128),
        viscosity.reshape(256, 128),
        inv_density,
        elem_group,
        coarse,
        cy, bz, cp, spr,
    )
    return new.reshape(fields.shape), pressure.reshape(viscosity.shape)


def build(mesh, nxc):
    placed = (
        P(None, "gx", None, "gy", None, None),
        P("gx", None, "gy", None, None),
        P("gx", "gy", None),
        P("gx", "gy", None),
        P(("gx", "gy"), None),
    )
    return jax.shard_map(
        functools.partial(per_device, mesh.shape["gx"], mesh.shape["gy"], nxc),
        mesh=mesh,
        in_specs=placed,
        out_specs=(P(None, "gx", None, "gy", None, None), P("gx", None, "gy", None, None)),
        check_vma=False,
    )


def solution(mesh):
    return build(mesh, XC)
```

```python
import functools

import jax
import jax.numpy as jnp
import numpy as np
from jax import lax
from jax.experimental import pallas as pl
from jax.experimental.pallas import tpu as pltpu
from jax.sharding import PartitionSpec as P

NCD = 4
XC = 8
YL = 8

dt_step = 0.01
sigma_p = 4.0
prandtl = 0.7
cheb_ratio = 0.1

F32 = jnp.float32
BF16 = jnp.bfloat16
DIRS = [(-1, 0), (1, 0), (0, -1), (0, 1), (-1, -1), (-1, 1), (1, -1), (1, 1)]
MESH = pl.DeviceIdType.MESH


def tables():
    points = np.array(
        [
            -1.0,
            -0.8717401485096066,
            -0.5917001814331423,
            -0.2092992179024789,
            0.2092992179024789,
            0.5917001814331423,
            0.8717401485096066,
            1.0,
        ]
    )
    weights = np.array(
        [
            1.0 / 28.0,
            0.2107042271435061,
            0.3411226924835044,
            0.4124587946587038,
            0.4124587946587038,
            0.3411226924835044,
            0.2107042271435061,
            1.0 / 28.0,
        ]
    )
    identity = np.eye(8)
    differ = points[:, None] - points[None, :] + identity
    barycentric = 1.0 / np.prod(differ, axis=1)
    offdiag = barycentric[None, :] / barycentric[:, None] / differ * (1.0 - identity)
    derivative = offdiag - identity * np.sum(offdiag, axis=1)[:, None]
    mass_one = identity * weights[None, :]
    stiff_one = derivative.T @ mass_one @ derivative
    stiff_three = (
        np.kron(np.kron(stiff_one, mass_one), mass_one)
        + np.kron(np.kron(mass_one, stiff_one), mass_one)
        + np.kron(np.kron(mass_one, mass_one), stiff_one)
    )
    three_diag = np.sum(stiff_three * np.eye(512), axis=1)
    spectral_bound = float(np.max(np.sum(np.abs(stiff_three), axis=1) / three_diag))
    return derivative, weights, stiff_one, spectral_bound


DER, WTS, STF, SBOUND = tables()
KLN = np.diag(STF)


def functionals():
    count = 8
    found = []
    for first in (3, 0, count - 2):
        both = np.zeros((2, 6, 16))
        mult = np.ones((count, 8))
        mult[1:, 0] = 2.0
        mult[:-1, 7] = 2.0
        for place in range(6):
            e = first - 2 + place
            if not 0 <= e < count:
                continue
            phi = np.zeros((count, 8))
            phi[e] = 1.0 / mult[e]
            if e > 0:
                phi[e - 1, 7] = phi[e, 0]
            if e < count - 1:
                phi[e + 1, 0] = phi[e, 7]
            t = -(phi * WTS[None, :]) @ DER
            joint = t[:-1, 7] + t[1:, 0]
            t[:-1, 7] = joint
            t[1:, 0] = joint
            t = t / (mult * WTS[None, :])
            both[0, place] = t[first : first + 2].reshape(16)
            both[1, place] = phi[first : first + 2].reshape(16)
        found.append(both)
    return np.stack(found, 0)


def z_functional():
    mult = np.ones((16, 8))
    mult[1:, 0] = 2.0
    mult[:-1, 7] = 2.0
    full = np.zeros((128, 128))
    for e in range(16):
        phi = np.zeros((16, 8))
        phi[e] = 1.0 / mult[e]
        if e > 0:
            phi[e - 1, 7] = phi[e, 0]
        if e < 15:
            phi[e + 1, 0] = phi[e, 7]
        t = -(phi * WTS[None, :]) @ DER
        joint = t[:-1, 7] + t[1:, 0]
        t[:-1, 7] = joint
        t[1:, 0] = joint
        t = t / (mult * WTS[None, :])
        full[:, 8 * e : 8 * e + 8] = t.reshape(128)[:, None] / 8.0
    return full


FUN = functionals()


def constants():
    cols = np.stack([DER, DER.T, STF], 0)
    cy = np.broadcast_to(np.transpose(cols, (0, 2, 1))[:, :, :, None], (3, 8, 8, 128))

    def big(one):
        full = (one if one.shape[0] == 128 else np.kron(np.eye(16), one)).astype(np.float32)
        high = np.asarray(full, dtype=jnp.bfloat16)
        low = np.asarray(full - high.astype(np.float32), dtype=jnp.bfloat16)
        return np.block([[high, low], [high, np.zeros_like(low)]])

    bz = np.stack([big(DER.T), big(DER), big(STF), big(z_functional())], 0)
    wy = np.tile(WTS, 2)[:, None]
    ky = np.tile(KLN, 2)[:, None]
    wz = np.tile(WTS, 16)[None, :]
    kz = np.tile(KLN, 16)[None, :]
    one = np.ones((16, 128))
    cp = np.stack([wy * wz, one * wz, wy * one, ky * wz + wy * kz, 1.0 / (wy * wz)], 0)
    spread = np.kron(np.eye(16), np.ones((1, 8)))
    fy = np.stack([FUN[0], FUN[1] - FUN[0], FUN[2] - FUN[0]], 0).reshape(36, 16)
    fy = np.broadcast_to(fy[:, :, None], (36, 16, 128))
    return (
        jnp.asarray(np.ascontiguousarray(cy), F32),
        jnp.asarray(bz, BF16),
        jnp.asarray(cp, F32),
        jnp.asarray(spread, F32),
        jnp.asarray(np.ascontiguousarray(fy), F32),
    )


def kernel(
    nx, ny, nxc,
    fields, visc, dens_h, grp_h, coarse, cy_h, bz_h, cp_h, spr_h, fy_h,
    out_f, out_p,
    dens, grp, cy, bz, cp, spr, fy, YF, G, TR,
    F, FN, V, L4, L1, W, IM, KAP, INVD, CX, AUX, AUXR, OH, PC,
    T1, T2, T3, R0, S0, Z0, W1, ZI,
    sx4, sy4, sc4, rx4, ry4, rc4, sx1, sy1, sc1, rx1, ry1, rc1,
    ag1, ag3,
    s_sem, r_sem, as_sem, ar_sem, cs_sem, cr_sem, gs_sem, gr_sem, l_sem,
):
    gx = lax.axis_index("gx")
    gy = lax.axis_index("gy")
    nz = nx // nxc
    xc = gx % nxc
    zc = gx // nxc

    def nbr(dx, dy):
        return ((gx + dx + nx) % nx, (gy + dy + ny) % ny)

    def z_mate(k):
        return (((zc + k) % nz) * nxc + xc, gy)

    def hops(off):
        dx, dy = off
        chips = dx // 2
        return min(chips, nxc // 2 - chips) + min(dy, ny - dy)

    flat = [(dx, dy) for dx in range(nxc) for dy in range(ny)][1:]
    flat.sort(key=hops, reverse=True)
    zline = sorted(range(1, nz), key=lambda k: -min(k, nz - k))

    def p_mate(dx, dy):
        return (zc * nxc + (xc + dx) % nxc, (gy + dy) % ny)

    mates = [nbr(dx, dy) for dx, dy in DIRS if dx != 0]
    mates += [p_mate(*off) for off in flat]
    mates += [z_mate(k) for k in zline]
    if nxc * ny < 4:
        mates += [nbr(0, -1), nbr(0, 1)]
    barrier = pltpu.get_barrier_semaphore()
    for mate in mates:
        pl.semaphore_signal(barrier, inc=1, device_id=mate, device_id_type=MESH)

    load_f = []
    for c in range(4):
        part = pl.ds(256 * c, 256)
        load_f.append(pltpu.make_async_copy(fields.at[part], F.at[part], l_sem.at[c]))
    small = [(dens_h, dens), (grp_h, grp), (spr_h, spr), (cp_h, cp)]
    large = [(cy_h, cy), (bz_h, bz), (visc, V), (fy_h, fy)]
    load_s = [
        pltpu.make_async_copy(src, dst, l_sem.at[4 + k]) for k, (src, dst) in enumerate(small)
    ]
    load_l = [
        pltpu.make_async_copy(src, dst, l_sem.at[8 + k]) for k, (src, dst) in enumerate(large)
    ]
    load_c = pltpu.make_async_copy(coarse, CX.at[8], l_sem.at[12])
    for copy in load_f + load_s + load_l + [load_c]:
        copy.start()

    lane = lax.broadcasted_iota(jnp.int32, (8, 128), 1)
    sub = lax.broadcasted_iota(jnp.int32, (8, 128), 0)
    one = jnp.float32(1.0)
    zero = jnp.float32(0.0)
    j7 = jnp.where((lane % 8 == 7) & (lane < 127), one, zero)
    j0 = jnp.where((lane % 8 == 0) & (lane > 0), one, zero)
    j7p = jnp.concatenate([j7, j7], 0)
    j0p = jnp.concatenate([j0, j0], 0)
    s0 = jnp.where(sub == 0, one, zero)
    s7 = jnp.where(sub == 7, one, zero)

    has_l = jnp.where(gx > 0, one, zero)
    has_r = jnp.where(gx < nx - 1, one, zero)
    has_b = jnp.where(gy > 0, one, zero)
    has_t = jnp.where(gy < ny - 1, one, zero)
    vx = {-1: has_l, 0: one, 1: has_r}
    vy = {-1: has_b, 0: one, 1: has_t}

    def zjoin(v):
        return v + j7p * pltpu.roll(v, 127, 1) + j0p * pltpu.roll(v, 1, 1)

    def rows(x, base=0):
        return pl.ds(base + 16 * x, 16)

    def xyjoin(L, base=0):
        both = L[pl.ds(base + 112, 16), :] + L[pl.ds(base + 128, 16), :]
        L[pl.ds(base + 112, 16), :] = both
        L[pl.ds(base + 128, 16), :] = both
        pair = L[pl.ds(base + 7, 16, stride=16), :] + L[pl.ds(base + 8, 16, stride=16), :]
        L[pl.ds(base + 7, 16, stride=16), :] = pair
        L[pl.ds(base + 8, 16, stride=16), :] = pair

    def yop(plane, which):
        parts = []
        for t in range(2):
            tile = plane[8 * t : 8 * t + 8, :]
            total = None
            for b in range(8):
                term = jnp.broadcast_to(tile[b : b + 1, :], (8, 128)) * cy[which, b]
                total = term if total is None else total + term
            parts.append(total)
        return jnp.concatenate(parts, 0)

    def xop(planes, coef):
        total = None
        for a in range(8):
            term = planes[a] * jnp.float32(coef[a])
            total = term if total is None else total + term
        return total

    def zop(f, which):
        high = f.astype(BF16)
        low = (f - high.astype(F32)).astype(BF16)
        both = jnp.concatenate([high, low], 1)
        prod = jnp.dot(both, bz[which], preferred_element_type=F32)
        return prod[:, :128] + prod[:, 128:]

    def faces(L, nch, e, sx, sy, sc, rx, ry, rc, num):
        for c in range(nch):
            base = 256 * c
            sx[e, 0, pl.ds(16 * c, 16), :] = L[pl.ds(base, 16), :]
            sx[e, 1, pl.ds(16 * c, 16), :] = L[pl.ds(base + 240, 16), :]
            sy[e, 0, pl.ds(16 * c, 16), :] = L[pl.ds(base, 16, stride=16), :]
            sy[e, 1, pl.ds(16 * c, 16), :] = L[pl.ds(base + 15, 16, stride=16), :]
            for k, (dx, dy) in enumerate(DIRS[4:]):
                row = base + (240 if dx > 0 else 0) + (15 if dy > 0 else 0)
                sc[e, k, pl.ds(c, 1), :] = L[pl.ds(row, 1), :]
        copies = []
        for d in (4, 5, 6, 7, 0, 1, 2, 3):
            if d < 2:
                src, dst = sx.at[e, d], rx.at[e, d]
            elif d < 4:
                src, dst = sy.at[e, d - 2], ry.at[e, d - 2]
            else:
                src, dst = sc.at[e, d - 4], rc.at[e, d - 4]
            copy = pltpu.make_async_remote_copy(
                src, dst, s_sem.at[num, d], r_sem.at[num, d],
                device_id=nbr(*DIRS[d]), device_id_type=MESH,
            )
            copy.start()
            copies.append(copy)
        return copies

    def finish(copies, L, nch, e, rx, ry, rc):
        for copy in copies:
            copy.wait_recv()
        for c in range(nch):
            base = 256 * c
            at = pl.ds(16 * c, 16)
            lo, hi = pl.ds(base, 16), pl.ds(base + 240, 16)
            L[lo, :] = L[lo, :] + has_l * rx[e, 1, at, :]
            L[hi, :] = L[hi, :] + has_r * rx[e, 0, at, :]
            lo, hi = pl.ds(base, 16, stride=16), pl.ds(base + 15, 16, stride=16)
            L[lo, :] = L[lo, :] + has_b * ry[e, 1, at, :]
            L[hi, :] = L[hi, :] + has_t * ry[e, 0, at, :]
            for k, (dx, dy) in enumerate(DIRS[4:]):
                row = pl.ds(base + (0 if dx > 0 else 240) + (0 if dy > 0 else 15), 1)
                L[row, :] = L[row, :] + (vx[-dx] * vy[-dy]) * rc[e, k, pl.ds(c, 1), :]

    set4 = (sx4, sy4, sc4, rx4, ry4, rc4)
    set1 = (sx1, sy1, sc1, rx1, ry1, rc1)
    pending = []

    for c in range(4):
        load_f[c].wait()
        for x in range(16):
            L4[rows(x, 256 * c), :] = zjoin(F[rows(x, 256 * c), :])
        xyjoin(L4, 256 * c)
    pl.semaphore_wait(barrier, len(mates))
    now = faces(L4, 4, 0, *set4, 0)
    pending += now
    for copy in load_s:
        copy.wait()
    for ex in range(2):
        AUX[pl.ds(2 * ex, 2), :] = jnp.dot(
            dens[ex], spr[...], preferred_element_type=F32, precision=lax.Precision.HIGHEST
        )
        AUX[pl.ds(4 + 2 * ex, 2), :] = jnp.dot(
            grp[ex].astype(F32), spr[...], preferred_element_type=F32,
            precision=lax.Precision.HIGHEST,
        )
    for ex in range(2):
        for ey in range(2):
            row = AUX[pl.ds(2 * ex + ey, 1), :]
            KAP[pl.ds(16 * ex + 8 * ey, 8), :] = jnp.broadcast_to(row, (8, 128))

    side = []
    for d, (dx, dy) in enumerate(DIRS):
        copy = pltpu.make_async_remote_copy(
            AUX, AUXR.at[d], as_sem.at[d], ar_sem.at[d],
            device_id=nbr(dx, dy), device_id_type=MESH,
        )
        copy.start()
        side.append(copy)
    rowsc = []
    for d, (dx, dy) in enumerate(DIRS):
        copy = pltpu.make_async_remote_copy(
            coarse, CX.at[d], cs_sem.at[d], cr_sem.at[d],
            device_id=nbr(dx, dy), device_id_type=MESH,
        )
        copy.start()
        rowsc.append(copy)

    half = jnp.float32(0.5)
    imx = [one] * 16
    imx[0] = jnp.where(gx > 0, half, one)
    imx[7] = imx[8] = half
    imx[15] = jnp.where(gx < nx - 1, half, one)
    imz = one - half * (j7 + j0)
    imy0 = one - half * s7 - (half * has_b) * s0
    imy1 = one - half * s0 - (half * has_t) * s7
    imyz = jnp.concatenate([imy0 * imz, imy1 * imz], 0)
    for x in range(16):
        W[rows(x), :] = jnp.float32(WTS[x % 8]) * cp[0]
        IM[rows(x), :] = imx[x] * imyz

    for copy in load_l + [load_c]:
        copy.wait()
    V[...] = V[...] * W[...]
    no_b, no_t = one - has_b, one - has_t
    for k in range(12):
        YF[k] = fy[k] + no_b * fy[12 + k] + no_t * fy[24 + k]
    finish(now, L4, 4, 0, rx4, ry4, rc4)
    for c in range(4):
        at = pl.ds(256 * c, 256)
        F[at, :] = L4[at, :] * IM[...]

    for copy in side:
        copy.wait_recv()

    def where_from(ex, ey):
        return ex // 2 - 1, ey // 2 - 1, 2 * (ex % 2) + ey % 2

    def slot_of(dx, dy):
        return 8 if (dx, dy) == (0, 0) else DIRS.index((-dx, -dy))

    around = [
        (ex, ey) for ex in range(6) for ey in range(6) if not (ex in (0, 5) and ey in (0, 5))
    ]
    kgrid = [[None] * 4 for _ in range(4)]
    for ex, ey in around:
        dx, dy, local = where_from(ex, ey)
        slot = slot_of(dx, dy)
        valid = vx[dx] * vy[dy]
        if slot == 8:
            krow = AUX[pl.ds(local, 1), :]
            grow = AUX[pl.ds(4 + local, 1), :]
        else:
            krow = AUXR[slot, pl.ds(local, 1), :]
            grow = AUXR[slot, pl.ds(4 + local, 1), :]
        if 1 <= ex <= 4 and 1 <= ey <= 4:
            kgrid[ex - 1][ey - 1] = krow * valid
        hit = jnp.abs(jnp.broadcast_to(grow, (4, 128)) - sub[0:4].astype(F32)) < half
        OH[6 * ex + ey] = jnp.where(hit, valid, zero)

    def channel(c, carry):
        base = pl.multiple_of(c * 256, 256)
        coef = jnp.where(c == 3, jnp.float32(1.0 / prandtl), one)
        T3[...] = zop(F[pl.ds(base, 256), :], 0)
        for ex in range(2):
            planes = [F[pl.ds(base + 16 * (8 * ex + a), 16), :] for a in range(8)]
            for i in range(8):
                x = 8 * ex + i
                gxp = xop(planes, DER[i])
                gyp = yop(planes[i], 0)
                gzp = T3[rows(x), :]
                adv = (
                    F[rows(x), :] * gxp + F[rows(x, 256), :] * gyp + F[rows(x, 512), :] * gzp
                )
                nuw = coef * V[rows(x), :]
                T1[rows(x), :] = nuw * gxp
                T2[rows(x), :] = yop(nuw * gyp, 1) + W[rows(x), :] * adv
                T3[rows(x), :] = nuw * gzp
        T3[...] = zop(T3[...], 1) + T2[...]
        for ex in range(2):
            planes = [T1[rows(8 * ex + a), :] for a in range(8)]
            for i in range(8):
                x = 8 * ex + i
                total = xop(planes, DER[:, i]) + T3[rows(x), :]
                at = pl.ds(base + 16 * x, 16)
                G[at, :] = W[rows(x), :] * F[at, :] - jnp.float32(dt_step) * total
                L4[at, :] = zjoin(-total)
        xyjoin(L4, base)
        return carry

    lax.fori_loop(0, 4, channel, 0)
    now = faces(L4, 4, 1, *set4, 1)
    pending += now

    group = lane[0:1] // 32
    parts = [jnp.where(group == g, one, zero) for g in range(4)]

    def ag_start(a, row):
        ag1[a, xc, 0] = row
        out = []
        for dx, dy in flat:
            copy = pltpu.make_async_remote_copy(
                ag1.at[a, xc, 0], ag1.at[a, xc, dy],
                gs_sem.at[a, dx * ny + dy], gr_sem.at[a, dx * ny + dy],
                device_id=p_mate(dx, dy), device_id_type=MESH,
            )
            copy.start()
            out.append(copy)
        return out

    def ag_second(a, copies, only_sums=False):
        for copy in copies:
            copy.wait_recv()
        pre = [[None] * 3 for _ in range(4)]
        for xs in range(nxc):
            row = ag1[a, xs, 0]
            for k in range(1, ny):
                row = row + ag1[a, xs, k]
            for g in range(3, 4) if only_sums else range(4):
                t = xs + g - 1
                if g == 3:
                    row_at, to_at = 2, 1
                elif t < 0:
                    row_at, to_at = 2, 3
                elif t > nxc - 1:
                    row_at, to_at = 2, 0
                else:
                    row_at, to_at = t // 4, t % 4
                turn = (to_at - g) % 4
                part = row * parts[g]
                old = pre[turn][row_at]
                pre[turn][row_at] = part if old is None else old + part
        blank = jnp.zeros((1, 128), F32)
        message = None
        for turn in range(4):
            if all(row is None for row in pre[turn]):
                continue
            block = [blank if row is None else row for row in pre[turn]] + [blank] * 5
            block = jnp.concatenate(block, 0)
            if turn:
                block = pltpu.roll(block, 32 * turn, 1)
            message = block if message is None else message + block
        ag3[a, zc] = message[0:4]
        out = []
        for k in zline:
            copy = pltpu.make_async_remote_copy(
                ag3.at[a, zc], ag3.at[a, zc], gs_sem.at[a, 64 + k], gr_sem.at[a, 64 + k],
                device_id=z_mate(k), device_id_type=MESH,
            )
            copy.start()
            out.append(copy)
        return out

    def ag_end(a, copies):
        for copy in copies:
            copy.wait_recv()

    def sums(a, count):
        total = ag3[a, 0][2:3]
        for z in range(1, nz):
            total = total + ag3[a, z][2:3]
        lanes = lane[0:1]
        return [
            jnp.sum(jnp.where(lanes == 32 + k, total, zero), axis=1, keepdims=True)
            for k in range(count)
        ]

    devs = [(dx, dy) for dx in (-1, 0, 1) for dy in (-1, 0, 1)]
    members = {dev: [] for dev in devs}
    for ex, ey in around:
        dx, dy, _ = where_from(ex, ey)
        members[(dx, dy)].append((ex, ey))

    def restricted(L):
        x_first = imx[0] * L[rows(0), :]
        x_last = imx[15] * L[rows(15), :]
        low, high = x_first, x_last
        for x in range(1, 7):
            low = low + L[rows(x), :]
            high = high + L[rows(x + 8), :]
        low = low + half * L[rows(7), :]
        high = high + half * L[rows(8), :]
        grid = {}
        for ex, part in enumerate((x_first, low, high, x_last)):
            part = part * imyz
            t0, t1 = part[0:8], part[8:16]
            grid[ex + 1, 1] = t0[0:1]
            grid[ex + 1, 2] = jnp.sum(t0, axis=0, keepdims=True)
            grid[ex + 1, 3] = jnp.sum(t1, axis=0, keepdims=True)
            grid[ex + 1, 4] = t1[7:8]
        return share(grid)

    def share(grid):
        message = jnp.zeros((4, 128), F32)
        for dx, dy in devs:
            acc = None
            for ex, ey in members[(dx, dy)]:
                if (ex, ey) not in grid:
                    continue
                term = jnp.broadcast_to(grid[ex, ey], (4, 128)) * OH[6 * ex + ey]
                acc = term if acc is None else acc + term
            value = jnp.sum(acc, axis=1, keepdims=True)
            to = 32 * (dx + 1) + ((gy + dy + YL) % YL) * NCD + sub[0:4]
            message = message + jnp.where(lane[0:4] == to, value, zero)
        return jnp.sum(message, axis=0, keepdims=True)

    def along(table, ex, x):
        c0 = FUN[0, table, ex, x]
        cl, cr = FUN[1, table, ex, x] - c0, FUN[2, table, ex, x] - c0
        if max(abs(c0), abs(cl), abs(cr)) < 1e-12:
            return None
        value = jnp.float32(c0)
        if abs(cl) > 1e-12:
            value = value + jnp.float32(cl) * (one - has_l)
        if abs(cr) > 1e-12:
            value = value + jnp.float32(cr) * (one - has_r)
        return value

    def restricted_early():
        TR[...] = jnp.zeros((2, 40, 128), F32)
        for ex in range(6):
            summed = []
            for c, table in ((0, 0), (1, 1), (2, 1)):
                total = None
                for x in range(16):
                    coef = along(table, ex, x)
                    if coef is None:
                        continue
                    term = coef * G[rows(x, 256 * c), :]
                    total = term if total is None else total + term
                summed.append(total)
            for ey in range(6):
                if (ex, ey) not in around:
                    continue
                at = pl.ds(6 * ex + ey, 1)
                value = None
                if 1 <= ey <= 4:
                    value = YF[6 + ey] * summed[0]
                if 1 <= ex <= 4:
                    term = YF[ey] * summed[1]
                    value = term if value is None else value + term
                TR[0, at, :] = jnp.sum(value, axis=0, keepdims=True)
                if 1 <= ex <= 4 and 1 <= ey <= 4:
                    TR[1, at, :] = jnp.sum(YF[6 + ey] * summed[2], axis=0, keepdims=True)
        last = zop(TR[1], 3)
        grid = {}
        for tile in range(5):
            v = TR[0, pl.ds(8 * tile, 8), :] * imz
            v = v + j7 * pltpu.roll(v, 127, 1) + j0 * pltpu.roll(v, 1, 1)
            v = v + last[8 * tile : 8 * tile + 8]
            for k in range(8):
                if (8 * tile + k) // 6 < 6 and divmod(8 * tile + k, 6) in around:
                    grid[divmod(8 * tile + k, 6)] = v[k : k + 1]
        return share(grid)

    def with_sums(row, values):
        lanes = lane[0:1]
        for k, value in enumerate(values):
            row = row + jnp.where(lanes == 96 + k, value, zero)
        return row

    ga = ag_start(0, restricted_early())
    pend_g = list(ga)

    xsets = [(0, 1), (1,), (1, 2), (2,), (2, 3)]
    xclass = [0] + [1] * 6 + [2, 2] + [3] * 6 + [4]

    def spread(grid):
        planes = []
        for members in xsets:
            e = []
            for ey in range(4):
                total = grid[members[0]][ey]
                for ex in members[1:]:
                    total = total + grid[ex][ey]
                e.append(jnp.broadcast_to(total, (8, 128)))
            low = e[1] + s0 * e[0] + s7 * e[2]
            high = e[2] + s0 * e[1] + s7 * e[3]
            planes.append(zjoin(jnp.concatenate([low, high], 0)))
        return planes

    kplanes = spread(kgrid)
    mult = one / imyz
    for x in range(16):
        wa = jnp.float32(WTS[x % 8])
        ka = jnp.float32(KLN[x % 8])
        diag = (ka * cp[0] + wa * cp[3]) * kplanes[xclass[x]] + (
            jnp.float32(sigma_p) * wa / imx[x]
        ) * cp[0] * mult
        INVD[rows(x), :] = one / diag

    def coarse_planes(a):
        lanes = lane[0:1]
        accs = [None] * 9
        for z in range(nz):
            own = ag3[a, z]
            first, second = own[0:1], own[1:2]
            if z > 0:
                first = first + jnp.where(lanes < 32, ag3[a, z - 1][2:3], zero)
            if z < nz - 1:
                second = second + jnp.where(lanes >= 96, ag3[a, z + 1][2:3], zero)
            for h, part in enumerate((first, second)):
                wide = jnp.broadcast_to(part, (4, 128))
                for n in range(9):
                    term = CX[n, :, pl.ds((2 * z + h) * 128, 128)] * wide
                    accs[n] = term if accs[n] is None else accs[n] + term
        values = [jnp.sum(acc, axis=1, keepdims=True) for acc in accs]
        grid = []
        for ex in range(4):
            line = []
            for ey in range(4):
                dx, dy, _ = where_from(ex + 1, ey + 1)
                value = values[slot_of(dx, dy)]
                line.append(jnp.sum(OH[6 * ex + ey + 7] * value, axis=0, keepdims=True))
            grid.append(line)
        return [plane * imyz for plane in spread(grid)]

    def apply_local(q, put):
        T3[...] = zop(q[...], 2)
        for ex in range(2):
            planes = [q[rows(8 * ex + a), :] for a in range(8)]
            kap = KAP[pl.ds(16 * ex, 16), :]
            for i in range(8):
                x = 8 * ex + i
                wa = jnp.float32(WTS[i])
                kx = xop(planes, STF[i])
                ky = yop(planes[i], 2)
                inner = cp[0] * kx + wa * (cp[1] * ky + cp[2] * T3[rows(x), :])
                put(x, planes[i], kap * inner + (jnp.float32(sigma_p) * wa) * (cp[0] * planes[i]))

    def put_joined(x, plane, value):
        L1[rows(x), :] = zjoin(value)

    upper = SBOUND
    lower = cheb_ratio * upper
    theta = 0.5 * (upper + lower)
    delta = 0.5 * (upper - lower)
    rho = delta / theta
    rho_next = 1.0 / (2.0 * theta / delta - rho)
    c2 = 2.0 * rho_next / delta
    c1 = jnp.float32((1.0 + rho_next * rho) / theta + c2)
    c2 = jnp.float32(c2 / theta)

    finish(now, L4, 4, 1, rx4, ry4, rc4)
    for x in range(16):
        scale = (jnp.float32(dt_step / WTS[x % 8]) * imx[x]) * (imyz * cp[4])
        for c in range(4):
            at = rows(x, 256 * c)
            FN[at, :] = F[at, :] + L4[at, :] * scale
    store_f = pltpu.make_async_copy(FN, out_f, l_sem.at[13])
    store_f.start()
    T3[...] = zop(FN[pl.ds(512, 256), :], 0)
    for ex in range(2):
        planes = [FN[rows(8 * ex + a), :] for a in range(8)]
        for i in range(8):
            x = 8 * ex + i
            div = xop(planes, DER[i]) + yop(FN[rows(x, 256), :], 0) + T3[rows(x), :]
            L1[rows(x), :] = zjoin(-(W[rows(x), :] * div))
    xyjoin(L1)

    now = faces(L1, 1, 0, *set1, 2)
    pending += now
    ga = ag_second(0, ga)
    pend_g += ga
    finish(now, L1, 1, 0, rx1, ry1, rc1)
    R0[...] = L1[...]
    T1[...] = L1[...] * INVD[...]
    apply_local(T1, put_joined)
    xyjoin(L1)
    now = faces(L1, 1, 1, *set1, 3)
    pending += now
    finish(now, L1, 1, 1, rx1, ry1, rc1)
    S0[...] = c1 * T1[...] - c2 * (INVD[...] * L1[...])
    for copy in rowsc:
        copy.wait_recv()
    ag_end(0, ga)
    planes = coarse_planes(0)
    for x in range(16):
        Z0[rows(x), :] = S0[rows(x), :] + imx[x] * planes[xclass[x]]

    dot = []

    def put_first(x, plane, value):
        W1[rows(x), :] = value
        L1[rows(x), :] = zjoin(value)
        term = plane * value
        dot.append(term if not dot else dot.pop() + term)

    def full(v):
        return jnp.sum(jnp.sum(v, axis=0, keepdims=True), axis=1, keepdims=True)

    apply_local(Z0, put_first)
    xyjoin(L1)
    rz_part = None
    for x in range(16):
        term = imx[x] * (R0[rows(x), :] * Z0[rows(x), :])
        rz_part = term if rz_part is None else rz_part + term
    row = with_sums(restricted(L1), [full(rz_part * imyz), full(dot.pop())])
    ga = ag_start(1, row)
    pend_g += ga
    now = faces(L1, 1, 2, *set1, 4)
    pending += now
    finish(now, L1, 1, 2, rx1, ry1, rc1)
    T2[...] = L1[...]
    T1[...] = L1[...] * INVD[...]
    apply_local(T1, put_joined)
    xyjoin(L1)
    now = faces(L1, 1, 3, *set1, 5)
    pending += now
    ga = ag_second(1, ga)
    pend_g += ga
    finish(now, L1, 1, 3, rx1, ry1, rc1)
    ZI[...] = c1 * T1[...] - c2 * (INVD[...] * L1[...])
    ag_end(1, ga)
    rz0, curv0 = sums(1, 2)
    step0 = rz0 / curv0
    planes = coarse_planes(1)
    rz_part = None
    for x in range(16):
        at = rows(x)
        zi = ZI[at, :] + imx[x] * planes[xclass[x]]
        z1 = Z0[at, :] - step0 * zi
        ZI[at, :] = z1
        term = imx[x] * ((R0[at, :] - step0 * T2[at, :]) * z1)
        rz_part = term if rz_part is None else rz_part + term

    dots = [None, None]

    def put_second(x, plane, value):
        terms = (plane * value, Z0[rows(x), :] * value + plane * W1[rows(x), :])
        for k in range(2):
            dots[k] = terms[k] if dots[k] is None else dots[k] + terms[k]

    apply_local(ZI, put_second)
    row = with_sums(
        jnp.zeros((1, 128), F32), [full(rz_part * imyz), full(dots[0]), full(dots[1])]
    )
    ga = ag_start(2, row)
    pend_g += ga
    ga = ag_second(2, ga, True)
    pend_g += ga
    ag_end(2, ga)
    rz1, a11, a10 = sums(2, 3)
    beta = rz1 / rz0
    curv1 = a11 + beta * a10 + beta * beta * curv0
    step1 = rz1 / curv1
    PC[...] = (step0 + step1 * beta) * Z0[...] + step1 * ZI[...]
    store_p = pltpu.make_async_copy(PC, out_p, l_sem.at[14])
    store_p.start()

    for copy in pending + side + rowsc + pend_g:
        copy.wait_send()
    store_f.wait()
    store_p.wait()


def per_device(nx, ny, nxc, fields, viscosity, inv_density, elem_group, coarse_inverse):
    nz = nx // nxc
    cy, bz, cp, spr, fy = constants()
    coarse = coarse_inverse
    if nxc * ny != XC * YL:
        coarse = coarse.reshape(NCD, nz, nxc, ny, NCD)
        coarse = jnp.pad(coarse, ((0, 0), (0, 0), (0, XC - nxc), (0, YL - ny), (0, 0)))
        coarse = coarse.reshape(NCD, nz * XC * YL * NCD)
    ncp = coarse.shape[1]

    def vm(*shape):
        return pltpu.VMEM(shape, F32)

    field = vm(256, 128)
    scratch = [
        vm(2, 2, 16), pltpu.VMEM((2, 2, 16), jnp.int32), vm(3, 8, 8, 128),
        pltpu.VMEM((4, 256, 256), BF16), vm(5, 16, 128), vm(16, 128), vm(36, 16, 128),
        vm(12, 16, 128), vm(1024, 128), vm(2, 40, 128),
        vm(1024, 128), vm(1024, 128), field, vm(1024, 128), field, field, field,
        vm(32, 128), field, vm(9, NCD, ncp), vm(8, 128), vm(8, 8, 128), vm(36, 4, 128), field,
        field, field, field, field, field, field, field, field,
        vm(2, 2, 64, 128), vm(2, 2, 64, 128), vm(2, 4, 4, 128),
        vm(2, 2, 64, 128), vm(2, 2, 64, 128), vm(2, 4, 4, 128),
        vm(4, 2, 16, 128), vm(4, 2, 16, 128), vm(4, 4, 1, 128),
        vm(4, 2, 16, 128), vm(4, 2, 16, 128), vm(4, 4, 1, 128),
        vm(3, nxc, ny, 1, 128), vm(3, nz, 4, 128),
        pltpu.SemaphoreType.DMA((6, 8)), pltpu.SemaphoreType.DMA((6, 8)),
        pltpu.SemaphoreType.DMA((8,)), pltpu.SemaphoreType.DMA((8,)),
        pltpu.SemaphoreType.DMA((8,)), pltpu.SemaphoreType.DMA((8,)),
        pltpu.SemaphoreType.DMA((3, 76)), pltpu.SemaphoreType.DMA((3, 76)),
        pltpu.SemaphoreType.DMA((15,)),
    ]
    anywhere = pl.BlockSpec(memory_space=pl.ANY)
    new, pressure = pl.pallas_call(
        functools.partial(kernel, nx, ny, nxc),
        out_shape=(
            jax.ShapeDtypeStruct((1024, 128), F32),
            jax.ShapeDtypeStruct((256, 128), F32),
        ),
        in_specs=[pl.BlockSpec(memory_space=pltpu.HBM)] * 10,
        out_specs=(anywhere, anywhere),
        scratch_shapes=scratch,
        compiler_params=pltpu.CompilerParams(
            collective_id=0, has_side_effects=True, vmem_limit_bytes=24 << 20
        ),
    )(
        *[pltpu.with_memory_space_constraint(v, pltpu.HBM) for v in (
        fields.reshape(1024, 128),
        viscosity.reshape(256, 128),
        inv_density,
        elem_group,
        coarse,
        cy, bz, cp, spr, fy)],
    )
    return new.reshape(fields.shape), pressure.reshape(viscosity.shape)


def build(mesh, nxc):
    placed = (
        P(None, "gx", None, "gy", None, None),
        P("gx", None, "gy", None, None),
        P("gx", "gy", None),
        P("gx", "gy", None),
        P(("gx", "gy"), None),
    )
    return jax.shard_map(
        functools.partial(per_device, mesh.shape["gx"], mesh.shape["gy"], nxc),
        mesh=mesh,
        in_specs=placed,
        out_specs=(P(None, "gx", None, "gy", None, None), P("gx", None, "gy", None, None)),
        check_vma=False,
    )


def solution(mesh):
    return build(mesh, XC)
```

```python
import functools

import jax
import jax.numpy as jnp
import numpy as np
from jax import lax
from jax.experimental import pallas as pl
from jax.experimental.pallas import tpu as pltpu
from jax.sharding import PartitionSpec as P

NCD = 4
XC = 8
YL = 8

dt_step = 0.01
sigma_p = 4.0
prandtl = 0.7
cheb_ratio = 0.1

F32 = jnp.float32
BF16 = jnp.bfloat16
DIRS = [(-1, 0), (1, 0), (0, -1), (0, 1), (-1, -1), (-1, 1), (1, -1), (1, 1)]
MESH = pl.DeviceIdType.MESH


def tables():
    points = np.array(
        [
            -1.0,
            -0.8717401485096066,
            -0.5917001814331423,
            -0.2092992179024789,
            0.2092992179024789,
            0.5917001814331423,
            0.8717401485096066,
            1.0,
        ]
    )
    weights = np.array(
        [
            1.0 / 28.0,
            0.2107042271435061,
            0.3411226924835044,
            0.4124587946587038,
            0.4124587946587038,
            0.3411226924835044,
            0.2107042271435061,
            1.0 / 28.0,
        ]
    )
    identity = np.eye(8)
    differ = points[:, None] - points[None, :] + identity
    barycentric = 1.0 / np.prod(differ, axis=1)
    offdiag = barycentric[None, :] / barycentric[:, None] / differ * (1.0 - identity)
    derivative = offdiag - identity * np.sum(offdiag, axis=1)[:, None]
    mass_one = identity * weights[None, :]
    stiff_one = derivative.T @ mass_one @ derivative
    stiff_three = (
        np.kron(np.kron(stiff_one, mass_one), mass_one)
        + np.kron(np.kron(mass_one, stiff_one), mass_one)
        + np.kron(np.kron(mass_one, mass_one), stiff_one)
    )
    three_diag = np.sum(stiff_three * np.eye(512), axis=1)
    spectral_bound = float(np.max(np.sum(np.abs(stiff_three), axis=1) / three_diag))
    return derivative, weights, stiff_one, spectral_bound


DER, WTS, STF, SBOUND = tables()
KLN = np.diag(STF)


def functionals():
    count = 8
    found = []
    for first in (3, 0, count - 2):
        both = np.zeros((2, 6, 16))
        mult = np.ones((count, 8))
        mult[1:, 0] = 2.0
        mult[:-1, 7] = 2.0
        for place in range(6):
            e = first - 2 + place
            if not 0 <= e < count:
                continue
            phi = np.zeros((count, 8))
            phi[e] = 1.0 / mult[e]
            if e > 0:
                phi[e - 1, 7] = phi[e, 0]
            if e < count - 1:
                phi[e + 1, 0] = phi[e, 7]
            t = -(phi * WTS[None, :]) @ DER
            joint = t[:-1, 7] + t[1:, 0]
            t[:-1, 7] = joint
            t[1:, 0] = joint
            t = t / (mult * WTS[None, :])
            both[0, place] = t[first : first + 2].reshape(16)
            both[1, place] = phi[first : first + 2].reshape(16)
        found.append(both)
    return np.stack(found, 0)


def z_functional():
    mult = np.ones((16, 8))
    mult[1:, 0] = 2.0
    mult[:-1, 7] = 2.0
    full = np.zeros((128, 128))
    for e in range(16):
        phi = np.zeros((16, 8))
        phi[e] = 1.0 / mult[e]
        if e > 0:
            phi[e - 1, 7] = phi[e, 0]
        if e < 15:
            phi[e + 1, 0] = phi[e, 7]
        t = -(phi * WTS[None, :]) @ DER
        joint = t[:-1, 7] + t[1:, 0]
        t[:-1, 7] = joint
        t[1:, 0] = joint
        t = t / (mult * WTS[None, :])
        full[:, 8 * e : 8 * e + 8] = t.reshape(128)[:, None] / 8.0
    return full


FUN = functionals()


def constants():
    cols = np.stack([DER, DER.T, STF], 0)
    cy = np.broadcast_to(np.transpose(cols, (0, 2, 1))[:, :, :, None], (3, 8, 8, 128))

    def big(one):
        full = (one if one.shape[0] == 128 else np.kron(np.eye(16), one)).astype(np.float32)
        high = np.asarray(full, dtype=jnp.bfloat16)
        low = np.asarray(full - high.astype(np.float32), dtype=jnp.bfloat16)
        return np.block([[high, low], [high, np.zeros_like(low)]])

    bz = np.stack([big(DER.T), big(DER), big(STF), big(z_functional())], 0)
    wy = np.tile(WTS, 2)[:, None]
    ky = np.tile(KLN, 2)[:, None]
    wz = np.tile(WTS, 16)[None, :]
    kz = np.tile(KLN, 16)[None, :]
    one = np.ones((16, 128))
    cp = np.stack([wy * wz, one * wz, wy * one, ky * wz + wy * kz, 1.0 / (wy * wz)], 0)
    spread = np.kron(np.eye(16), np.ones((1, 8)))
    fy = np.stack([FUN[0], FUN[1] - FUN[0], FUN[2] - FUN[0]], 0).reshape(36, 16)
    fy = np.broadcast_to(fy[:, :, None], (36, 16, 128))
    return (
        jnp.asarray(np.ascontiguousarray(cy), F32),
        jnp.asarray(bz, BF16),
        jnp.asarray(cp, F32),
        jnp.asarray(spread, F32),
        jnp.asarray(np.ascontiguousarray(fy), F32),
    )


def kernel(
    nx, ny, nxc,
    fields, visc, dens_h, grp_h, coarse, cy_h, bz_h, cp_h, spr_h, fy_h,
    out_f, out_p,
    dens, grp, cy, bz, cp, spr, fy, YF, G, TR,
    F, FN, V, L4, L1, W, IM, KAP, INVD, CX, AUX, AUXR, OH, PC,
    T1, T2, T3, R0, S0, Z0, W1, ZI,
    sx4, sy4, sc4, rx4, ry4, rc4, sx1, sy1, sc1, rx1, ry1, rc1,
    ag1, ag3,
    s_sem, r_sem, as_sem, ar_sem, cs_sem, cr_sem, gs_sem, gr_sem, l_sem,
):
    gx = lax.axis_index("gx")
    gy = lax.axis_index("gy")
    nz = nx // nxc
    xc = gx % nxc
    zc = gx // nxc

    def nbr(dx, dy):
        return ((gx + dx + nx) % nx, (gy + dy + ny) % ny)

    def z_mate(k):
        return (((zc + k) % nz) * nxc + xc, gy)

    def hops(off):
        dx, dy = off
        chips = dx // 2
        return min(chips, nxc // 2 - chips) + min(dy, ny - dy)

    flat = [(dx, dy) for dx in range(nxc) for dy in range(ny)][1:]
    flat.sort(key=hops, reverse=True)
    zline = sorted(range(1, nz), key=lambda k: -min(k, nz - k))

    def p_mate(dx, dy):
        return (zc * nxc + (xc + dx) % nxc, (gy + dy) % ny)

    load_f = []
    for c in range(4):
        part = pl.ds(256 * c, 256)
        load_f.append(pltpu.make_async_copy(fields.at[part], F.at[part], l_sem.at[c]))
    small = [(dens_h, dens), (grp_h, grp), (spr_h, spr), (cp_h, cp)]
    large = [(cy_h, cy), (bz_h, bz), (visc, V), (fy_h, fy)]
    load_s = [
        pltpu.make_async_copy(src, dst, l_sem.at[4 + k]) for k, (src, dst) in enumerate(small)
    ]
    load_l = [
        pltpu.make_async_copy(src, dst, l_sem.at[8 + k]) for k, (src, dst) in enumerate(large)
    ]
    load_c = pltpu.make_async_copy(coarse, CX.at[8], l_sem.at[12])
    for copy in load_f + load_s + load_l + [load_c]:
        copy.start()

    ranked = [(hops(off), p_mate(*off)) for off in flat]
    ranked += [(min(k, nz - k), z_mate(k)) for k in zline]
    ranked += [(2 + abs(dy), nbr(dx, dy)) for dx, dy in DIRS if dx != 0 or nxc * ny < 4]
    ranked.sort(key=lambda item: -item[0])
    mates = [mate for _, mate in ranked]
    barrier = pltpu.get_barrier_semaphore()
    for mate in mates:
        pl.semaphore_signal(barrier, inc=1, device_id=mate, device_id_type=MESH)

    lane = lax.broadcasted_iota(jnp.int32, (8, 128), 1)
    sub = lax.broadcasted_iota(jnp.int32, (8, 128), 0)
    one = jnp.float32(1.0)
    zero = jnp.float32(0.0)
    j7 = jnp.where((lane % 8 == 7) & (lane < 127), one, zero)
    j0 = jnp.where((lane % 8 == 0) & (lane > 0), one, zero)
    j7p = jnp.concatenate([j7, j7], 0)
    j0p = jnp.concatenate([j0, j0], 0)
    s0 = jnp.where(sub == 0, one, zero)
    s7 = jnp.where(sub == 7, one, zero)

    has_l = jnp.where(gx > 0, one, zero)
    has_r = jnp.where(gx < nx - 1, one, zero)
    has_b = jnp.where(gy > 0, one, zero)
    has_t = jnp.where(gy < ny - 1, one, zero)
    vx = {-1: has_l, 0: one, 1: has_r}
    vy = {-1: has_b, 0: one, 1: has_t}

    def zjoin(v):
        return v + j7p * pltpu.roll(v, 127, 1) + j0p * pltpu.roll(v, 1, 1)

    def rows(x, base=0):
        return pl.ds(base + 16 * x, 16)

    def xyjoin(L, base=0):
        both = L[pl.ds(base + 112, 16), :] + L[pl.ds(base + 128, 16), :]
        L[pl.ds(base + 112, 16), :] = both
        L[pl.ds(base + 128, 16), :] = both
        pair = L[pl.ds(base + 7, 16, stride=16), :] + L[pl.ds(base + 8, 16, stride=16), :]
        L[pl.ds(base + 7, 16, stride=16), :] = pair
        L[pl.ds(base + 8, 16, stride=16), :] = pair

    def yop(plane, which):
        parts = []
        for t in range(2):
            tile = plane[8 * t : 8 * t + 8, :]
            total = None
            for b in range(8):
                term = jnp.broadcast_to(tile[b : b + 1, :], (8, 128)) * cy[which, b]
                total = term if total is None else total + term
            parts.append(total)
        return jnp.concatenate(parts, 0)

    def xop(planes, matrix, sign):
        even = [planes[a] + planes[7 - a] for a in range(4)]
        odd = [planes[a] - planes[7 - a] for a in range(4)]
        out = [None] * 8
        for i in range(4):
            p = q = None
            for a in range(4):
                both = even[a] * jnp.float32((matrix[i, a] + matrix[i, 7 - a]) / 2)
                diff = odd[a] * jnp.float32((matrix[i, a] - matrix[i, 7 - a]) / 2)
                p = both if p is None else p + both
                q = diff if q is None else q + diff
            out[i] = p + q
            out[7 - i] = p - q if sign > 0 else q - p
        return out

    def zop(f, which):
        high = f.astype(BF16)
        low = (f - high.astype(F32)).astype(BF16)
        both = jnp.concatenate([high, low], 1)
        prod = jnp.dot(both, bz[which], preferred_element_type=F32)
        return prod[:, :128] + prod[:, 128:]

    def faces(L, nch, e, sx, sy, sc, rx, ry, rc, num, start=0):
        used = pl.ds(0, 16 * nch)
        for c in range(nch):
            base = start + 256 * c
            sx[e, 0, pl.ds(16 * c, 16), :] = L[pl.ds(base, 16), :]
            sx[e, 1, pl.ds(16 * c, 16), :] = L[pl.ds(base + 240, 16), :]
            sy[e, 0, pl.ds(16 * c, 16), :] = L[pl.ds(base, 16, stride=16), :]
            sy[e, 1, pl.ds(16 * c, 16), :] = L[pl.ds(base + 15, 16, stride=16), :]
            for k, (dx, dy) in enumerate(DIRS[4:]):
                row = base + (240 if dx > 0 else 0) + (15 if dy > 0 else 0)
                sc[e, k, pl.ds(c, 1), :] = L[pl.ds(row, 1), :]
        copies = []
        for d in (4, 5, 6, 7, 0, 1, 2, 3):
            if d < 2:
                src, dst = sx.at[e, d, used], rx.at[e, d, used]
            elif d < 4:
                src, dst = sy.at[e, d - 2, used], ry.at[e, d - 2, used]
            else:
                src, dst = sc.at[e, d - 4], rc.at[e, d - 4]
            copy = pltpu.make_async_remote_copy(
                src, dst, s_sem.at[num, d], r_sem.at[num, d],
                device_id=nbr(*DIRS[d]), device_id_type=MESH,
            )
            copy.start()
            copies.append(copy)
        return copies

    def finish(copies, L, nch, e, rx, ry, rc, start=0):
        for copy in copies:
            copy.wait_recv()
        for c in range(nch):
            base = start + 256 * c
            at = pl.ds(16 * c, 16)
            lo, hi = pl.ds(base, 16), pl.ds(base + 240, 16)
            L[lo, :] = L[lo, :] + has_l * rx[e, 1, at, :]
            L[hi, :] = L[hi, :] + has_r * rx[e, 0, at, :]
            lo, hi = pl.ds(base, 16, stride=16), pl.ds(base + 15, 16, stride=16)
            L[lo, :] = L[lo, :] + has_b * ry[e, 1, at, :]
            L[hi, :] = L[hi, :] + has_t * ry[e, 0, at, :]
            for k, (dx, dy) in enumerate(DIRS[4:]):
                row = pl.ds(base + (0 if dx > 0 else 240) + (0 if dy > 0 else 15), 1)
                L[row, :] = L[row, :] + (vx[-dx] * vy[-dy]) * rc[e, k, pl.ds(c, 1), :]

    set4 = (sx4, sy4, sc4, rx4, ry4, rc4)
    set1 = (sx1, sy1, sc1, rx1, ry1, rc1)
    pending = []

    for c in range(4):
        load_f[c].wait()
        for x in range(16):
            L4[rows(x, 256 * c), :] = zjoin(F[rows(x, 256 * c), :])
        xyjoin(L4, 256 * c)
    pl.semaphore_wait(barrier, len(mates))
    now = faces(L4, 4, 0, *set4, 0)
    pending += now
    for copy in load_s:
        copy.wait()
    for ex in range(2):
        AUX[pl.ds(2 * ex, 2), :] = jnp.dot(
            dens[ex], spr[...], preferred_element_type=F32, precision=lax.Precision.HIGHEST
        )
        AUX[pl.ds(4 + 2 * ex, 2), :] = jnp.dot(
            grp[ex].astype(F32), spr[...], preferred_element_type=F32,
            precision=lax.Precision.HIGHEST,
        )
    for ex in range(2):
        for ey in range(2):
            row = AUX[pl.ds(2 * ex + ey, 1), :]
            KAP[pl.ds(16 * ex + 8 * ey, 8), :] = jnp.broadcast_to(row, (8, 128))

    side = []
    for d, (dx, dy) in enumerate(DIRS):
        copy = pltpu.make_async_remote_copy(
            AUX, AUXR.at[d], as_sem.at[d], ar_sem.at[d],
            device_id=nbr(dx, dy), device_id_type=MESH,
        )
        copy.start()
        side.append(copy)
    rowsc = []
    for d, (dx, dy) in enumerate(DIRS):
        copy = pltpu.make_async_remote_copy(
            coarse, CX.at[d], cs_sem.at[d], cr_sem.at[d],
            device_id=nbr(dx, dy), device_id_type=MESH,
        )
        copy.start()
        rowsc.append(copy)

    half = jnp.float32(0.5)
    imx = [one] * 16
    imx[0] = jnp.where(gx > 0, half, one)
    imx[7] = imx[8] = half
    imx[15] = jnp.where(gx < nx - 1, half, one)
    imz = one - half * (j7 + j0)
    imy0 = one - half * s7 - (half * has_b) * s0
    imy1 = one - half * s0 - (half * has_t) * s7
    imyz = jnp.concatenate([imy0 * imz, imy1 * imz], 0)
    for x in range(16):
        W[rows(x), :] = jnp.float32(WTS[x % 8]) * cp[0]
        IM[rows(x), :] = imx[x] * imyz

    for copy in load_l + [load_c]:
        copy.wait()
    V[...] = V[...] * W[...]
    no_b, no_t = one - has_b, one - has_t
    for k in range(12):
        YF[k] = fy[k] + no_b * fy[12 + k] + no_t * fy[24 + k]
    finish(now, L4, 4, 0, rx4, ry4, rc4)
    for c in range(4):
        at = pl.ds(256 * c, 256)
        F[at, :] = L4[at, :] * IM[...]

    for copy in side:
        copy.wait_recv()

    def where_from(ex, ey):
        return ex // 2 - 1, ey // 2 - 1, 2 * (ex % 2) + ey % 2

    def slot_of(dx, dy):
        return 8 if (dx, dy) == (0, 0) else DIRS.index((-dx, -dy))

    around = [
        (ex, ey) for ex in range(6) for ey in range(6) if not (ex in (0, 5) and ey in (0, 5))
    ]
    kgrid = [[None] * 4 for _ in range(4)]
    for ex, ey in around:
        dx, dy, local = where_from(ex, ey)
        slot = slot_of(dx, dy)
        valid = vx[dx] * vy[dy]
        if slot == 8:
            krow = AUX[pl.ds(local, 1), :]
            grow = AUX[pl.ds(4 + local, 1), :]
        else:
            krow = AUXR[slot, pl.ds(local, 1), :]
            grow = AUXR[slot, pl.ds(4 + local, 1), :]
        if 1 <= ex <= 4 and 1 <= ey <= 4:
            kgrid[ex - 1][ey - 1] = krow * valid
        hit = jnp.abs(jnp.broadcast_to(grow, (4, 128)) - sub[0:4].astype(F32)) < half
        OH[6 * ex + ey] = jnp.where(hit, valid, zero)

    def channel(c, carry):
        if isinstance(c, int):
            base, coef = c * 256, jnp.float32(1.0 / prandtl)
        else:
            base, coef = pl.multiple_of(c * 256, 256), one
        T3[...] = zop(F[pl.ds(base, 256), :], 0)
        for ex in range(2):
            planes = [F[pl.ds(base + 16 * (8 * ex + a), 16), :] for a in range(8)]
            slopes = xop(planes, DER, -1)
            for i in range(8):
                x = 8 * ex + i
                gxp = slopes[i]
                gyp = yop(planes[i], 0)
                gzp = T3[rows(x), :]
                adv = (
                    F[rows(x), :] * gxp + F[rows(x, 256), :] * gyp + F[rows(x, 512), :] * gzp
                )
                nuw = coef * V[rows(x), :]
                T1[rows(x), :] = nuw * gxp
                T2[rows(x), :] = yop(nuw * gyp, 1) + W[rows(x), :] * adv
                T3[rows(x), :] = nuw * gzp
        T3[...] = zop(T3[...], 1) + T2[...]
        for ex in range(2):
            turned = xop([T1[rows(8 * ex + a), :] for a in range(8)], DER.T, -1)
            for i in range(8):
                x = 8 * ex + i
                total = turned[i] + T3[rows(x), :]
                at = pl.ds(base + 16 * x, 16)
                if not isinstance(c, int):
                    G[at, :] = W[rows(x), :] * F[at, :] - jnp.float32(dt_step) * total
                L4[at, :] = zjoin(-total)
        xyjoin(L4, base)
        return carry

    lax.fori_loop(0, 3, channel, 0)
    for k in range(4):
        sc4[1, k, pl.ds(3, 1), :] = jnp.zeros((1, 128), F32)
    now = faces(L4, 3, 1, *set4, 1)
    pending += now

    group = lane[0:1] // 32
    parts = [jnp.where(group == g, one, zero) for g in range(4)]

    def ag_start(a, row):
        ag1[a, xc, 0] = row
        out = []
        for dx, dy in flat:
            copy = pltpu.make_async_remote_copy(
                ag1.at[a, xc, 0], ag1.at[a, xc, dy],
                gs_sem.at[a, dx * ny + dy], gr_sem.at[a, dx * ny + dy],
                device_id=p_mate(dx, dy), device_id_type=MESH,
            )
            copy.start()
            out.append(copy)
        return out

    def ag_second(a, copies, only_sums=False):
        for copy in copies:
            copy.wait_recv()
        pre = [[None] * 3 for _ in range(4)]
        for xs in range(nxc):
            row = ag1[a, xs, 0]
            for k in range(1, ny):
                row = row + ag1[a, xs, k]
            for g in range(3, 4) if only_sums else range(4):
                t = xs + g - 1
                if g == 3:
                    row_at, to_at = 2, 1
                elif t < 0:
                    row_at, to_at = 2, 3
                elif t > nxc - 1:
                    row_at, to_at = 2, 0
                else:
                    row_at, to_at = t // 4, t % 4
                turn = (to_at - g) % 4
                part = row * parts[g]
                old = pre[turn][row_at]
                pre[turn][row_at] = part if old is None else old + part
        blank = jnp.zeros((1, 128), F32)
        message = None
        for turn in range(4):
            if all(row is None for row in pre[turn]):
                continue
            block = [blank if row is None else row for row in pre[turn]] + [blank] * 5
            block = jnp.concatenate(block, 0)
            if turn:
                block = pltpu.roll(block, 32 * turn, 1)
            message = block if message is None else message + block
        ag3[a, zc] = message[0:4]
        out = []
        for k in zline:
            copy = pltpu.make_async_remote_copy(
                ag3.at[a, zc], ag3.at[a, zc], gs_sem.at[a, 64 + k], gr_sem.at[a, 64 + k],
                device_id=z_mate(k), device_id_type=MESH,
            )
            copy.start()
            out.append(copy)
        return out

    def ag_end(a, copies):
        for copy in copies:
            copy.wait_recv()

    def sums(a, count):
        total = ag3[a, 0][2:3]
        for z in range(1, nz):
            total = total + ag3[a, z][2:3]
        lanes = lane[0:1]
        return [
            jnp.sum(jnp.where(lanes == 32 + k, total, zero), axis=1, keepdims=True)
            for k in range(count)
        ]

    devs = [(dx, dy) for dx in (-1, 0, 1) for dy in (-1, 0, 1)]
    members = {dev: [] for dev in devs}
    for ex, ey in around:
        dx, dy, _ = where_from(ex, ey)
        members[(dx, dy)].append((ex, ey))

    def restricted(L):
        x_first = imx[0] * L[rows(0), :]
        x_last = imx[15] * L[rows(15), :]
        low, high = x_first, x_last
        for x in range(1, 7):
            low = low + L[rows(x), :]
            high = high + L[rows(x + 8), :]
        low = low + half * L[rows(7), :]
        high = high + half * L[rows(8), :]
        grid = {}
        for ex, part in enumerate((x_first, low, high, x_last)):
            part = part * imyz
            t0, t1 = part[0:8], part[8:16]
            grid[ex + 1, 1] = t0[0:1]
            grid[ex + 1, 2] = jnp.sum(t0, axis=0, keepdims=True)
            grid[ex + 1, 3] = jnp.sum(t1, axis=0, keepdims=True)
            grid[ex + 1, 4] = t1[7:8]
        return share(grid)

    def share(grid):
        message = jnp.zeros((4, 128), F32)
        for dx, dy in devs:
            acc = None
            for ex, ey in members[(dx, dy)]:
                if (ex, ey) not in grid:
                    continue
                term = jnp.broadcast_to(grid[ex, ey], (4, 128)) * OH[6 * ex + ey]
                acc = term if acc is None else acc + term
            value = jnp.sum(acc, axis=1, keepdims=True)
            to = 32 * (dx + 1) + ((gy + dy + YL) % YL) * NCD + sub[0:4]
            message = message + jnp.where(lane[0:4] == to, value, zero)
        return jnp.sum(message, axis=0, keepdims=True)

    def along(table, ex, x):
        c0 = FUN[0, table, ex, x]
        cl, cr = FUN[1, table, ex, x] - c0, FUN[2, table, ex, x] - c0
        if max(abs(c0), abs(cl), abs(cr)) < 1e-12:
            return None
        value = jnp.float32(c0)
        if abs(cl) > 1e-12:
            value = value + jnp.float32(cl) * (one - has_l)
        if abs(cr) > 1e-12:
            value = value + jnp.float32(cr) * (one - has_r)
        return value

    def restricted_early():
        TR[...] = jnp.zeros((2, 40, 128), F32)
        for ex in range(6):
            summed = []
            for c, table in ((0, 0), (1, 1), (2, 1)):
                total = None
                for x in range(16):
                    coef = along(table, ex, x)
                    if coef is None:
                        continue
                    term = coef * G[rows(x, 256 * c), :]
                    total = term if total is None else total + term
                summed.append(total)
            for ey in range(6):
                if (ex, ey) not in around:
                    continue
                at = pl.ds(6 * ex + ey, 1)
                value = None
                if 1 <= ey <= 4:
                    value = YF[6 + ey] * summed[0]
                if 1 <= ex <= 4:
                    term = YF[ey] * summed[1]
                    value = term if value is None else value + term
                TR[0, at, :] = jnp.sum(value, axis=0, keepdims=True)
                if 1 <= ex <= 4 and 1 <= ey <= 4:
                    TR[1, at, :] = jnp.sum(YF[6 + ey] * summed[2], axis=0, keepdims=True)
        last = zop(TR[1], 3)
        grid = {}
        for tile in range(5):
            v = TR[0, pl.ds(8 * tile, 8), :] * imz
            v = v + j7 * pltpu.roll(v, 127, 1) + j0 * pltpu.roll(v, 1, 1)
            v = v + last[8 * tile : 8 * tile + 8]
            for k in range(8):
                if (8 * tile + k) // 6 < 6 and divmod(8 * tile + k, 6) in around:
                    grid[divmod(8 * tile + k, 6)] = v[k : k + 1]
        return share(grid)

    def with_sums(row, values):
        lanes = lane[0:1]
        for k, value in enumerate(values):
            row = row + jnp.where(lanes == 96 + k, value, zero)
        return row

    ga = ag_start(0, restricted_early())
    pend_g = list(ga)
    channel(3, 0)
    warm = faces(L4, 1, 4, *set1, 6, start=768)
    pending += warm

    xsets = [(0, 1), (1,), (1, 2), (2,), (2, 3)]
    xclass = [0] + [1] * 6 + [2, 2] + [3] * 6 + [4]

    def spread(grid):
        planes = []
        for members in xsets:
            e = []
            for ey in range(4):
                total = grid[members[0]][ey]
                for ex in members[1:]:
                    total = total + grid[ex][ey]
                e.append(jnp.broadcast_to(total, (8, 128)))
            low = e[1] + s0 * e[0] + s7 * e[2]
            high = e[2] + s0 * e[1] + s7 * e[3]
            planes.append(zjoin(jnp.concatenate([low, high], 0)))
        return planes

    kplanes = spread(kgrid)
    mult = one / imyz
    for x in range(16):
        wa = jnp.float32(WTS[x % 8])
        ka = jnp.float32(KLN[x % 8])
        diag = (ka * cp[0] + wa * cp[3]) * kplanes[xclass[x]] + (
            jnp.float32(sigma_p) * wa / imx[x]
        ) * cp[0] * mult
        INVD[rows(x), :] = one / diag

    def coarse_planes(a):
        lanes = lane[0:1]
        accs = [None] * 9
        for z in range(nz):
            own = ag3[a, z]
            first, second = own[0:1], own[1:2]
            if z > 0:
                first = first + jnp.where(lanes < 32, ag3[a, z - 1][2:3], zero)
            if z < nz - 1:
                second = second + jnp.where(lanes >= 96, ag3[a, z + 1][2:3], zero)
            for h, part in enumerate((first, second)):
                wide = jnp.broadcast_to(part, (4, 128))
                for n in range(9):
                    term = CX[n, :, pl.ds((2 * z + h) * 128, 128)] * wide
                    accs[n] = term if accs[n] is None else accs[n] + term
        values = [jnp.sum(acc, axis=1, keepdims=True) for acc in accs]
        grid = []
        for ex in range(4):
            line = []
            for ey in range(4):
                dx, dy, _ = where_from(ex + 1, ey + 1)
                value = values[slot_of(dx, dy)]
                line.append(jnp.sum(OH[6 * ex + ey + 7] * value, axis=0, keepdims=True))
            grid.append(line)
        return [plane * imyz for plane in spread(grid)]

    def apply_local(q, put):
        T3[...] = zop(q[...], 2)
        for ex in range(2):
            planes = [q[rows(8 * ex + a), :] for a in range(8)]
            stiff = xop(planes, STF, 1)
            kap = KAP[pl.ds(16 * ex, 16), :]
            for i in range(8):
                x = 8 * ex + i
                wa = jnp.float32(WTS[i])
                kx = stiff[i]
                ky = yop(planes[i], 2)
                inner = cp[0] * kx + wa * (cp[1] * ky + cp[2] * T3[rows(x), :])
                put(x, planes[i], kap * inner + (jnp.float32(sigma_p) * wa) * (cp[0] * planes[i]))

    def put_joined(x, plane, value):
        L1[rows(x), :] = zjoin(value)

    upper = SBOUND
    lower = cheb_ratio * upper
    theta = 0.5 * (upper + lower)
    delta = 0.5 * (upper - lower)
    rho = delta / theta
    rho_next = 1.0 / (2.0 * theta / delta - rho)
    c2 = 2.0 * rho_next / delta
    c1 = jnp.float32((1.0 + rho_next * rho) / theta + c2)
    c2 = jnp.float32(c2 / theta)

    def renew(channels):
        for x in range(16):
            scale = (jnp.float32(dt_step / WTS[x % 8]) * imx[x]) * (imyz * cp[4])
            for c in channels:
                at = rows(x, 256 * c)
                FN[at, :] = F[at, :] + L4[at, :] * scale

    finish(now, L4, 3, 1, rx4, ry4, rc4)
    renew(range(3))
    T3[...] = zop(FN[pl.ds(512, 256), :], 0)
    for ex in range(2):
        slopes = xop([FN[rows(8 * ex + a), :] for a in range(8)], DER, -1)
        for i in range(8):
            x = 8 * ex + i
            div = slopes[i] + yop(FN[rows(x, 256), :], 0) + T3[rows(x), :]
            L1[rows(x), :] = zjoin(-(W[rows(x), :] * div))
    xyjoin(L1)

    now = faces(L1, 1, 0, *set1, 2)
    pending += now
    ga = ag_second(0, ga)
    pend_g += ga
    finish(now, L1, 1, 0, rx1, ry1, rc1)
    R0[...] = L1[...]
    T1[...] = L1[...] * INVD[...]
    apply_local(T1, put_joined)
    xyjoin(L1)
    now = faces(L1, 1, 1, *set1, 3)
    pending += now
    finish(warm, L4, 1, 4, rx1, ry1, rc1, start=768)
    renew([3])
    store_f = pltpu.make_async_copy(FN, out_f, l_sem.at[13])
    store_f.start()
    finish(now, L1, 1, 1, rx1, ry1, rc1)
    S0[...] = c1 * T1[...] - c2 * (INVD[...] * L1[...])
    for copy in rowsc:
        copy.wait_recv()
    ag_end(0, ga)
    planes = coarse_planes(0)
    for x in range(16):
        Z0[rows(x), :] = S0[rows(x), :] + imx[x] * planes[xclass[x]]

    dot = []

    def put_first(x, plane, value):
        W1[rows(x), :] = value
        L1[rows(x), :] = zjoin(value)
        term = plane * value
        dot.append(term if not dot else dot.pop() + term)

    def full(v):
        return jnp.sum(jnp.sum(v, axis=0, keepdims=True), axis=1, keepdims=True)

    apply_local(Z0, put_first)
    xyjoin(L1)
    rz_part = None
    for x in range(16):
        term = imx[x] * (R0[rows(x), :] * Z0[rows(x), :])
        rz_part = term if rz_part is None else rz_part + term
    row = with_sums(restricted(L1), [full(rz_part * imyz), full(dot.pop())])
    ga = ag_start(1, row)
    pend_g += ga
    now = faces(L1, 1, 2, *set1, 4)
    pending += now
    finish(now, L1, 1, 2, rx1, ry1, rc1)
    T2[...] = L1[...]
    T1[...] = L1[...] * INVD[...]
    apply_local(T1, put_joined)
    xyjoin(L1)
    now = faces(L1, 1, 3, *set1, 5)
    pending += now
    ga = ag_second(1, ga)
    pend_g += ga
    finish(now, L1, 1, 3, rx1, ry1, rc1)
    ZI[...] = c1 * T1[...] - c2 * (INVD[...] * L1[...])
    ag_end(1, ga)
    rz0, curv0 = sums(1, 2)
    step0 = rz0 / curv0
    planes = coarse_planes(1)
    rz_part = None
    for x in range(16):
        at = rows(x)
        zi = ZI[at, :] + imx[x] * planes[xclass[x]]
        z1 = Z0[at, :] - step0 * zi
        ZI[at, :] = z1
        term = imx[x] * ((R0[at, :] - step0 * T2[at, :]) * z1)
        rz_part = term if rz_part is None else rz_part + term

    dots = [None, None]

    def put_second(x, plane, value):
        terms = (plane * value, Z0[rows(x), :] * value + plane * W1[rows(x), :])
        for k in range(2):
            dots[k] = terms[k] if dots[k] is None else dots[k] + terms[k]

    apply_local(ZI, put_second)
    row = with_sums(
        jnp.zeros((1, 128), F32), [full(rz_part * imyz), full(dots[0]), full(dots[1])]
    )
    ga = ag_start(2, row)
    for copy in pending + side + rowsc + pend_g:
        copy.wait_send()
    store_f.wait()
    for copy in ga:
        copy.wait_send()
    ga = ag_second(2, ga, True)
    for copy in ga:
        copy.wait_send()
    ag_end(2, ga)
    rz1, a11, a10 = sums(2, 3)
    beta = rz1 / rz0
    curv1 = a11 + beta * a10 + beta * beta * curv0
    step1 = rz1 / curv1
    PC[...] = (step0 + step1 * beta) * Z0[...] + step1 * ZI[...]
    store_p = pltpu.make_async_copy(PC, out_p, l_sem.at[14])
    store_p.start()

    store_p.wait()


def per_device(nx, ny, nxc, fields, viscosity, inv_density, elem_group, coarse_inverse):
    nz = nx // nxc
    cy, bz, cp, spr, fy = constants()
    coarse = coarse_inverse
    if nxc * ny != XC * YL:
        coarse = coarse.reshape(NCD, nz, nxc, ny, NCD)
        coarse = jnp.pad(coarse, ((0, 0), (0, 0), (0, XC - nxc), (0, YL - ny), (0, 0)))
        coarse = coarse.reshape(NCD, nz * XC * YL * NCD)
    ncp = coarse.shape[1]

    def vm(*shape):
        return pltpu.VMEM(shape, F32)

    field = vm(256, 128)
    scratch = [
        vm(2, 2, 16), pltpu.VMEM((2, 2, 16), jnp.int32), vm(3, 8, 8, 128),
        pltpu.VMEM((4, 256, 256), BF16), vm(5, 16, 128), vm(16, 128), vm(36, 16, 128),
        vm(12, 16, 128), vm(1024, 128), vm(2, 40, 128),
        vm(1024, 128), vm(1024, 128), field, vm(1024, 128), field, field, field,
        vm(32, 128), field, vm(9, NCD, ncp), vm(8, 128), vm(8, 8, 128), vm(36, 4, 128), field,
        field, field, field, field, field, field, field, field,
        vm(2, 2, 64, 128), vm(2, 2, 64, 128), vm(2, 4, 4, 128),
        vm(2, 2, 64, 128), vm(2, 2, 64, 128), vm(2, 4, 4, 128),
        vm(5, 2, 16, 128), vm(5, 2, 16, 128), vm(5, 4, 1, 128),
        vm(5, 2, 16, 128), vm(5, 2, 16, 128), vm(5, 4, 1, 128),
        vm(3, nxc, ny, 1, 128), vm(3, nz, 4, 128),
        pltpu.SemaphoreType.DMA((7, 8)), pltpu.SemaphoreType.DMA((7, 8)),
        pltpu.SemaphoreType.DMA((8,)), pltpu.SemaphoreType.DMA((8,)),
        pltpu.SemaphoreType.DMA((8,)), pltpu.SemaphoreType.DMA((8,)),
        pltpu.SemaphoreType.DMA((3, 76)), pltpu.SemaphoreType.DMA((3, 76)),
        pltpu.SemaphoreType.DMA((15,)),
    ]
    anywhere = pl.BlockSpec(memory_space=pl.ANY)
    new, pressure = pl.pallas_call(
        functools.partial(kernel, nx, ny, nxc),
        out_shape=(
            jax.ShapeDtypeStruct((1024, 128), F32),
            jax.ShapeDtypeStruct((256, 128), F32),
        ),
        in_specs=[pl.BlockSpec(memory_space=pltpu.HBM)] * 10,
        out_specs=(anywhere, anywhere),
        scratch_shapes=scratch,
        compiler_params=pltpu.CompilerParams(
            collective_id=0, has_side_effects=True, vmem_limit_bytes=24 << 20
        ),
    )(
        *[pltpu.with_memory_space_constraint(v, pltpu.HBM) for v in (
        fields.reshape(1024, 128),
        viscosity.reshape(256, 128),
        inv_density,
        elem_group,
        coarse,
        cy, bz, cp, spr, fy)],
    )
    return new.reshape(fields.shape), pressure.reshape(viscosity.shape)


def build(mesh, nxc):
    placed = (
        P(None, "gx", None, "gy", None, None),
        P("gx", None, "gy", None, None),
        P("gx", "gy", None),
        P("gx", "gy", None),
        P(("gx", "gy"), None),
    )
    return jax.shard_map(
        functools.partial(per_device, mesh.shape["gx"], mesh.shape["gy"], nxc),
        mesh=mesh,
        in_specs=placed,
        out_specs=(P(None, "gx", None, "gy", None, None), P("gx", None, "gy", None, None)),
        check_vma=False,
    )


def solution(mesh):
    return build(mesh, XC)
```

```python
import functools

import jax
import jax.numpy as jnp
import numpy as np
from jax import lax
from jax.experimental import pallas as pl
from jax.experimental.pallas import tpu as pltpu
from jax.sharding import PartitionSpec as P

NCD = 4
XC = 8
YL = 8

dt_step = 0.01
sigma_p = 4.0
prandtl = 0.7
cheb_ratio = 0.1

F32 = jnp.float32
BF16 = jnp.bfloat16
DIRS = [(-1, 0), (1, 0), (0, -1), (0, 1), (-1, -1), (-1, 1), (1, -1), (1, 1)]
MESH = pl.DeviceIdType.MESH


def tables():
    points = np.array(
        [
            -1.0,
            -0.8717401485096066,
            -0.5917001814331423,
            -0.2092992179024789,
            0.2092992179024789,
            0.5917001814331423,
            0.8717401485096066,
            1.0,
        ]
    )
    weights = np.array(
        [
            1.0 / 28.0,
            0.2107042271435061,
            0.3411226924835044,
            0.4124587946587038,
            0.4124587946587038,
            0.3411226924835044,
            0.2107042271435061,
            1.0 / 28.0,
        ]
    )
    identity = np.eye(8)
    differ = points[:, None] - points[None, :] + identity
    barycentric = 1.0 / np.prod(differ, axis=1)
    offdiag = barycentric[None, :] / barycentric[:, None] / differ * (1.0 - identity)
    derivative = offdiag - identity * np.sum(offdiag, axis=1)[:, None]
    mass_one = identity * weights[None, :]
    stiff_one = derivative.T @ mass_one @ derivative
    stiff_three = (
        np.kron(np.kron(stiff_one, mass_one), mass_one)
        + np.kron(np.kron(mass_one, stiff_one), mass_one)
        + np.kron(np.kron(mass_one, mass_one), stiff_one)
    )
    three_diag = np.sum(stiff_three * np.eye(512), axis=1)
    spectral_bound = float(np.max(np.sum(np.abs(stiff_three), axis=1) / three_diag))
    return derivative, weights, stiff_one, spectral_bound


DER, WTS, STF, SBOUND = tables()
KLN = np.diag(STF)


def functionals():
    count = 8
    found = []
    for first in (3, 0, count - 2):
        both = np.zeros((2, 6, 16))
        mult = np.ones((count, 8))
        mult[1:, 0] = 2.0
        mult[:-1, 7] = 2.0
        for place in range(6):
            e = first - 2 + place
            if not 0 <= e < count:
                continue
            phi = np.zeros((count, 8))
            phi[e] = 1.0 / mult[e]
            if e > 0:
                phi[e - 1, 7] = phi[e, 0]
            if e < count - 1:
                phi[e + 1, 0] = phi[e, 7]
            t = -(phi * WTS[None, :]) @ DER
            joint = t[:-1, 7] + t[1:, 0]
            t[:-1, 7] = joint
            t[1:, 0] = joint
            t = t / (mult * WTS[None, :])
            both[0, place] = t[first : first + 2].reshape(16)
            both[1, place] = phi[first : first + 2].reshape(16)
        found.append(both)
    return np.stack(found, 0)


def z_functional():
    mult = np.ones((16, 8))
    mult[1:, 0] = 2.0
    mult[:-1, 7] = 2.0
    full = np.zeros((128, 128))
    for e in range(16):
        phi = np.zeros((16, 8))
        phi[e] = 1.0 / mult[e]
        if e > 0:
            phi[e - 1, 7] = phi[e, 0]
        if e < 15:
            phi[e + 1, 0] = phi[e, 7]
        t = -(phi * WTS[None, :]) @ DER
        joint = t[:-1, 7] + t[1:, 0]
        t[:-1, 7] = joint
        t[1:, 0] = joint
        t = t / (mult * WTS[None, :])
        full[:, 8 * e : 8 * e + 8] = t.reshape(128)[:, None] / 8.0
    return full


FUN = functionals()


def constants():
    cols = np.stack([DER, DER.T, STF], 0)
    cy = np.broadcast_to(np.transpose(cols, (0, 2, 1))[:, :, :, None], (3, 8, 8, 128))

    def big(one):
        full = (one if one.shape[0] == 128 else np.kron(np.eye(16), one)).astype(np.float32)
        high = np.asarray(full, dtype=jnp.bfloat16)
        low = np.asarray(full - high.astype(np.float32), dtype=jnp.bfloat16)
        return np.block([[high, low], [high, np.zeros_like(low)]])

    bz = np.stack([big(DER.T), big(DER), big(STF), big(z_functional())], 0)
    wy = np.tile(WTS, 2)[:, None]
    ky = np.tile(KLN, 2)[:, None]
    wz = np.tile(WTS, 16)[None, :]
    kz = np.tile(KLN, 16)[None, :]
    one = np.ones((16, 128))
    cp = np.stack([wy * wz, one * wz, wy * one, ky * wz + wy * kz, 1.0 / (wy * wz)], 0)
    spread = np.kron(np.eye(16), np.ones((1, 8)))
    fy = np.stack([FUN[0], FUN[1] - FUN[0], FUN[2] - FUN[0]], 0).reshape(36, 16)
    fy = np.broadcast_to(fy[:, :, None], (36, 16, 128))
    return (
        jnp.asarray(np.ascontiguousarray(cy), F32),
        jnp.asarray(bz, BF16),
        jnp.asarray(cp, F32),
        jnp.asarray(spread, F32),
        jnp.asarray(np.ascontiguousarray(fy), F32),
    )


def kernel(
    nx, ny, nxc,
    fields, visc, dens_h, grp_h, coarse, cy_h, bz_h, cp_h, spr_h, fy_h,
    out_f, out_p,
    dens, grp, cy, bz, cp, spr, fy, YF, G, TR, C1, C2, C3, C4, W2,
    F, FN, V, L4, L1, W, IM, KAP, INVD, CX, AUX, AUXR, OH, PC,
    T1, T2, T3, R0, S0, Z0, W1, ZI,
    sx4, sy4, sc4, rx4, ry4, rc4, sx1, sy1, sc1, rx1, ry1, rc1,
    ag1, ag3,
    s_sem, r_sem, as_sem, ar_sem, cs_sem, cr_sem, gs_sem, gr_sem, l_sem,
):
    gx = lax.axis_index("gx")
    gy = lax.axis_index("gy")
    nz = nx // nxc
    xc = gx % nxc
    zc = gx // nxc

    def nbr(dx, dy):
        return ((gx + dx + nx) % nx, (gy + dy + ny) % ny)

    def z_mate(k):
        return (((zc + k) % nz) * nxc + xc, gy)

    def hops(off):
        dx, dy = off
        chips = dx // 2
        return min(chips, nxc // 2 - chips) + min(dy, ny - dy)

    flat = [(dx, dy) for dx in range(nxc) for dy in range(ny)][1:]
    flat.sort(key=hops, reverse=True)
    zline = sorted(range(1, nz), key=lambda k: -min(k, nz - k))

    def p_mate(dx, dy):
        return (zc * nxc + (xc + dx) % nxc, (gy + dy) % ny)

    load_f = []
    for c in range(4):
        part = pl.ds(256 * c, 256)
        load_f.append(pltpu.make_async_copy(fields.at[part], F.at[part], l_sem.at[c]))
    small = [(dens_h, dens), (grp_h, grp), (spr_h, spr), (cp_h, cp)]
    large = [(cy_h, cy), (bz_h, bz), (visc, V), (fy_h, fy)]
    load_s = [
        pltpu.make_async_copy(src, dst, l_sem.at[4 + k]) for k, (src, dst) in enumerate(small)
    ]
    load_l = [
        pltpu.make_async_copy(src, dst, l_sem.at[8 + k]) for k, (src, dst) in enumerate(large)
    ]
    load_c = pltpu.make_async_copy(coarse, CX.at[8], l_sem.at[12])
    for copy in load_f + load_s + load_l + [load_c]:
        copy.start()

    ranked = [(hops(off), p_mate(*off)) for off in flat]
    ranked += [(min(k, nz - k), z_mate(k)) for k in zline]
    ranked += [(2 + abs(dy), nbr(dx, dy)) for dx, dy in DIRS if dx != 0 or nxc * ny < 4]
    ranked.sort(key=lambda item: -item[0])
    mates = [mate for _, mate in ranked]
    barrier = pltpu.get_barrier_semaphore()
    for mate in mates:
        pl.semaphore_signal(barrier, inc=1, device_id=mate, device_id_type=MESH)

    lane = lax.broadcasted_iota(jnp.int32, (8, 128), 1)
    sub = lax.broadcasted_iota(jnp.int32, (8, 128), 0)
    one = jnp.float32(1.0)
    zero = jnp.float32(0.0)
    j7 = jnp.where((lane % 8 == 7) & (lane < 127), one, zero)
    j0 = jnp.where((lane % 8 == 0) & (lane > 0), one, zero)
    j7p = jnp.concatenate([j7, j7], 0)
    j0p = jnp.concatenate([j0, j0], 0)
    s0 = jnp.where(sub == 0, one, zero)
    s7 = jnp.where(sub == 7, one, zero)

    has_l = jnp.where(gx > 0, one, zero)
    has_r = jnp.where(gx < nx - 1, one, zero)
    has_b = jnp.where(gy > 0, one, zero)
    has_t = jnp.where(gy < ny - 1, one, zero)
    vx = {-1: has_l, 0: one, 1: has_r}
    vy = {-1: has_b, 0: one, 1: has_t}

    def zjoin(v):
        return v + j7p * pltpu.roll(v, 127, 1) + j0p * pltpu.roll(v, 1, 1)

    def rows(x, base=0):
        return pl.ds(base + 16 * x, 16)

    def xyjoin(L, base=0):
        both = L[pl.ds(base + 112, 16), :] + L[pl.ds(base + 128, 16), :]
        L[pl.ds(base + 112, 16), :] = both
        L[pl.ds(base + 128, 16), :] = both
        pair = L[pl.ds(base + 7, 16, stride=16), :] + L[pl.ds(base + 8, 16, stride=16), :]
        L[pl.ds(base + 7, 16, stride=16), :] = pair
        L[pl.ds(base + 8, 16, stride=16), :] = pair

    def yop(plane, which):
        parts = []
        for t in range(2):
            tile = plane[8 * t : 8 * t + 8, :]
            total = None
            for b in range(8):
                term = jnp.broadcast_to(tile[b : b + 1, :], (8, 128)) * cy[which, b]
                total = term if total is None else total + term
            parts.append(total)
        return jnp.concatenate(parts, 0)

    def xop(planes, matrix, sign):
        even = [planes[a] + planes[7 - a] for a in range(4)]
        odd = [planes[a] - planes[7 - a] for a in range(4)]
        out = [None] * 8
        for i in range(4):
            p = q = None
            for a in range(4):
                both = even[a] * jnp.float32((matrix[i, a] + matrix[i, 7 - a]) / 2)
                diff = odd[a] * jnp.float32((matrix[i, a] - matrix[i, 7 - a]) / 2)
                p = both if p is None else p + both
                q = diff if q is None else q + diff
            out[i] = p + q
            out[7 - i] = p - q if sign > 0 else q - p
        return out

    def zop(f, which):
        high = f.astype(BF16)
        low = (f - high.astype(F32)).astype(BF16)
        both = jnp.concatenate([high, low], 1)
        prod = jnp.dot(both, bz[which], preferred_element_type=F32)
        return prod[:, :128] + prod[:, 128:]

    def faces(L, nch, e, sx, sy, sc, rx, ry, rc, num, start=0):
        used = pl.ds(0, 16 * nch)
        for c in range(nch):
            base = start + 256 * c
            sx[e, 0, pl.ds(16 * c, 16), :] = L[pl.ds(base, 16), :]
            sx[e, 1, pl.ds(16 * c, 16), :] = L[pl.ds(base + 240, 16), :]
            sy[e, 0, pl.ds(16 * c, 16), :] = L[pl.ds(base, 16, stride=16), :]
            sy[e, 1, pl.ds(16 * c, 16), :] = L[pl.ds(base + 15, 16, stride=16), :]
            for k, (dx, dy) in enumerate(DIRS[4:]):
                row = base + (240 if dx > 0 else 0) + (15 if dy > 0 else 0)
                sc[e, k, pl.ds(c, 1), :] = L[pl.ds(row, 1), :]
        copies = []
        for d in (4, 5, 6, 7, 0, 1, 2, 3):
            if d < 2:
                src, dst = sx.at[e, d, used], rx.at[e, d, used]
            elif d < 4:
                src, dst = sy.at[e, d - 2, used], ry.at[e, d - 2, used]
            else:
                src, dst = sc.at[e, d - 4], rc.at[e, d - 4]
            copy = pltpu.make_async_remote_copy(
                src, dst, s_sem.at[num, d], r_sem.at[num, d],
                device_id=nbr(*DIRS[d]), device_id_type=MESH,
            )
            copy.start()
            copies.append(copy)
        return copies

    def finish(copies, L, nch, e, rx, ry, rc, start=0):
        for copy in copies:
            copy.wait_recv()
        for c in range(nch):
            base = start + 256 * c
            at = pl.ds(16 * c, 16)
            lo, hi = pl.ds(base, 16), pl.ds(base + 240, 16)
            L[lo, :] = L[lo, :] + has_l * rx[e, 1, at, :]
            L[hi, :] = L[hi, :] + has_r * rx[e, 0, at, :]
            lo, hi = pl.ds(base, 16, stride=16), pl.ds(base + 15, 16, stride=16)
            L[lo, :] = L[lo, :] + has_b * ry[e, 1, at, :]
            L[hi, :] = L[hi, :] + has_t * ry[e, 0, at, :]
            for k, (dx, dy) in enumerate(DIRS[4:]):
                row = pl.ds(base + (0 if dx > 0 else 240) + (0 if dy > 0 else 15), 1)
                L[row, :] = L[row, :] + (vx[-dx] * vy[-dy]) * rc[e, k, pl.ds(c, 1), :]

    set4 = (sx4, sy4, sc4, rx4, ry4, rc4)
    set1 = (sx1, sy1, sc1, rx1, ry1, rc1)
    pending = []

    for c in range(4):
        load_f[c].wait()
        for x in range(16):
            L4[rows(x, 256 * c), :] = zjoin(F[rows(x, 256 * c), :])
        xyjoin(L4, 256 * c)
    pl.semaphore_wait(barrier, len(mates))
    now = faces(L4, 4, 0, *set4, 0)
    pending += now
    for copy in load_s:
        copy.wait()
    for ex in range(2):
        AUX[pl.ds(2 * ex, 2), :] = jnp.dot(
            dens[ex], spr[...], preferred_element_type=F32, precision=lax.Precision.HIGHEST
        )
        AUX[pl.ds(4 + 2 * ex, 2), :] = jnp.dot(
            grp[ex].astype(F32), spr[...], preferred_element_type=F32,
            precision=lax.Precision.HIGHEST,
        )
    for ex in range(2):
        for ey in range(2):
            row = AUX[pl.ds(2 * ex + ey, 1), :]
            KAP[pl.ds(16 * ex + 8 * ey, 8), :] = jnp.broadcast_to(row, (8, 128))

    side = []
    for d, (dx, dy) in enumerate(DIRS):
        copy = pltpu.make_async_remote_copy(
            AUX, AUXR.at[d], as_sem.at[d], ar_sem.at[d],
            device_id=nbr(dx, dy), device_id_type=MESH,
        )
        copy.start()
        side.append(copy)
    rowsc = []
    for d, (dx, dy) in enumerate(DIRS):
        copy = pltpu.make_async_remote_copy(
            coarse, CX.at[d], cs_sem.at[d], cr_sem.at[d],
            device_id=nbr(dx, dy), device_id_type=MESH,
        )
        copy.start()
        rowsc.append(copy)

    half = jnp.float32(0.5)
    imx = [one] * 16
    imx[0] = jnp.where(gx > 0, half, one)
    imx[7] = imx[8] = half
    imx[15] = jnp.where(gx < nx - 1, half, one)
    imz = one - half * (j7 + j0)
    imy0 = one - half * s7 - (half * has_b) * s0
    imy1 = one - half * s0 - (half * has_t) * s7
    imyz = jnp.concatenate([imy0 * imz, imy1 * imz], 0)
    for x in range(16):
        W[rows(x), :] = jnp.float32(WTS[x % 8]) * cp[0]
        IM[rows(x), :] = imx[x] * imyz

    for copy in load_l + [load_c]:
        copy.wait()
    V[...] = V[...] * W[...]
    no_b, no_t = one - has_b, one - has_t
    for k in range(12):
        YF[k] = fy[k] + no_b * fy[12 + k] + no_t * fy[24 + k]
    finish(now, L4, 4, 0, rx4, ry4, rc4)
    for c in range(4):
        at = pl.ds(256 * c, 256)
        F[at, :] = L4[at, :] * IM[...]

    for copy in side:
        copy.wait_recv()

    def where_from(ex, ey):
        return ex // 2 - 1, ey // 2 - 1, 2 * (ex % 2) + ey % 2

    def slot_of(dx, dy):
        return 8 if (dx, dy) == (0, 0) else DIRS.index((-dx, -dy))

    around = [
        (ex, ey) for ex in range(6) for ey in range(6) if not (ex in (0, 5) and ey in (0, 5))
    ]
    kgrid = [[None] * 4 for _ in range(4)]
    for ex, ey in around:
        dx, dy, local = where_from(ex, ey)
        slot = slot_of(dx, dy)
        valid = vx[dx] * vy[dy]
        if slot == 8:
            krow = AUX[pl.ds(local, 1), :]
            grow = AUX[pl.ds(4 + local, 1), :]
        else:
            krow = AUXR[slot, pl.ds(local, 1), :]
            grow = AUXR[slot, pl.ds(4 + local, 1), :]
        if 1 <= ex <= 4 and 1 <= ey <= 4:
            kgrid[ex - 1][ey - 1] = krow * valid
        hit = jnp.abs(jnp.broadcast_to(grow, (4, 128)) - sub[0:4].astype(F32)) < half
        OH[6 * ex + ey] = jnp.where(hit, valid, zero)

    def channels(which):
        for c in which:
            at = pl.ds(256 * c, 256)
            C3[at, :] = zop(F[at, :], 0)
        for c in which:
            base = 256 * c
            coef = None if c < 3 else jnp.float32(1.0 / prandtl)
            for ex in range(2):
                planes = [F[rows(8 * ex + a, base), :] for a in range(8)]
                slopes = xop(planes, DER, -1)
                for i in range(8):
                    x = 8 * ex + i
                    gxp = slopes[i]
                    gyp = yop(planes[i], 0)
                    gzp = C3[rows(x, base), :]
                    adv = (
                        F[rows(x), :] * gxp + F[rows(x, 256), :] * gyp + F[rows(x, 512), :] * gzp
                    )
                    nuw = V[rows(x), :] if coef is None else coef * V[rows(x), :]
                    C1[rows(x, base), :] = nuw * gxp
                    C2[rows(x, base), :] = yop(nuw * gyp, 1) + W[rows(x), :] * adv
                    C4[rows(x, base), :] = nuw * gzp
            at = pl.ds(base, 256)
            C3[at, :] = zop(C4[at, :], 1)
        for c in which:
            base = 256 * c
            for ex in range(2):
                turned = xop([C1[rows(8 * ex + a, base), :] for a in range(8)], DER.T, -1)
                for i in range(8):
                    x = 8 * ex + i
                    at = rows(x, base)
                    total = turned[i] + (C3[at, :] + C2[at, :])
                    if c < 3:
                        G[at, :] = W[rows(x), :] * F[at, :] - jnp.float32(dt_step) * total
                    L4[at, :] = zjoin(-total)
            xyjoin(L4, base)

    channels(range(3))
    for k in range(4):
        sc4[1, k, pl.ds(3, 1), :] = jnp.zeros((1, 128), F32)
    now = faces(L4, 3, 1, *set4, 1)
    pending += now

    group = lane[0:1] // 32
    parts = [jnp.where(group == g, one, zero) for g in range(4)]

    def ag_start(a, row):
        ag1[a, xc, 0] = row
        out = []
        for dx, dy in flat:
            copy = pltpu.make_async_remote_copy(
                ag1.at[a, xc, 0], ag1.at[a, xc, dy],
                gs_sem.at[a, dx * ny + dy], gr_sem.at[a, dx * ny + dy],
                device_id=p_mate(dx, dy), device_id_type=MESH,
            )
            copy.start()
            out.append(copy)
        return out

    def ag_second(a, copies, only_sums=False):
        for copy in copies:
            copy.wait_recv()
        pre = [[None] * 3 for _ in range(4)]
        for xs in range(nxc):
            row = ag1[a, xs, 0]
            for k in range(1, ny):
                row = row + ag1[a, xs, k]
            for g in range(3, 4) if only_sums else range(4):
                t = xs + g - 1
                if g == 3:
                    row_at, to_at = 2, 1
                elif t < 0:
                    row_at, to_at = 2, 3
                elif t > nxc - 1:
                    row_at, to_at = 2, 0
                else:
                    row_at, to_at = t // 4, t % 4
                turn = (to_at - g) % 4
                part = row * parts[g]
                old = pre[turn][row_at]
                pre[turn][row_at] = part if old is None else old + part
        blank = jnp.zeros((1, 128), F32)
        message = None
        for turn in range(4):
            if all(row is None for row in pre[turn]):
                continue
            block = [blank if row is None else row for row in pre[turn]] + [blank] * 5
            block = jnp.concatenate(block, 0)
            if turn:
                block = pltpu.roll(block, 32 * turn, 1)
            message = block if message is None else message + block
        ag3[a, zc] = message[0:4]
        out = []
        for k in zline:
            copy = pltpu.make_async_remote_copy(
                ag3.at[a, zc], ag3.at[a, zc], gs_sem.at[a, 64 + k], gr_sem.at[a, 64 + k],
                device_id=z_mate(k), device_id_type=MESH,
            )
            copy.start()
            out.append(copy)
        return out

    def ag_end(a, copies):
        for copy in copies:
            copy.wait_recv()

    def sums(a, count):
        total = ag3[a, 0][2:3]
        for z in range(1, nz):
            total = total + ag3[a, z][2:3]
        lanes = lane[0:1]
        return [
            jnp.sum(jnp.where(lanes == 32 + k, total, zero), axis=1, keepdims=True)
            for k in range(count)
        ]

    devs = [(dx, dy) for dx in (-1, 0, 1) for dy in (-1, 0, 1)]
    members = {dev: [] for dev in devs}
    for ex, ey in around:
        dx, dy, _ = where_from(ex, ey)
        members[(dx, dy)].append((ex, ey))

    def restricted(L):
        x_first = imx[0] * L[rows(0), :]
        x_last = imx[15] * L[rows(15), :]
        low, high = x_first, x_last
        for x in range(1, 7):
            low = low + L[rows(x), :]
            high = high + L[rows(x + 8), :]
        low = low + half * L[rows(7), :]
        high = high + half * L[rows(8), :]
        grid = {}
        for ex, part in enumerate((x_first, low, high, x_last)):
            part = part * imyz
            t0, t1 = part[0:8], part[8:16]
            grid[ex + 1, 1] = t0[0:1]
            grid[ex + 1, 2] = jnp.sum(t0, axis=0, keepdims=True)
            grid[ex + 1, 3] = jnp.sum(t1, axis=0, keepdims=True)
            grid[ex + 1, 4] = t1[7:8]
        return share(grid)

    def share(grid):
        message = jnp.zeros((4, 128), F32)
        for dx, dy in devs:
            acc = None
            for ex, ey in members[(dx, dy)]:
                if (ex, ey) not in grid:
                    continue
                term = jnp.broadcast_to(grid[ex, ey], (4, 128)) * OH[6 * ex + ey]
                acc = term if acc is None else acc + term
            value = jnp.sum(acc, axis=1, keepdims=True)
            to = 32 * (dx + 1) + ((gy + dy + YL) % YL) * NCD + sub[0:4]
            message = message + jnp.where(lane[0:4] == to, value, zero)
        return jnp.sum(message, axis=0, keepdims=True)

    def along(table, ex, x):
        c0 = FUN[0, table, ex, x]
        cl, cr = FUN[1, table, ex, x] - c0, FUN[2, table, ex, x] - c0
        if max(abs(c0), abs(cl), abs(cr)) < 1e-12:
            return None
        value = jnp.float32(c0)
        if abs(cl) > 1e-12:
            value = value + jnp.float32(cl) * (one - has_l)
        if abs(cr) > 1e-12:
            value = value + jnp.float32(cr) * (one - has_r)
        return value

    def restricted_early():
        TR[...] = jnp.zeros((2, 40, 128), F32)
        for ex in range(6):
            summed = []
            for c, table in ((0, 0), (1, 1), (2, 1)):
                total = None
                for x in range(16):
                    coef = along(table, ex, x)
                    if coef is None:
                        continue
                    term = coef * G[rows(x, 256 * c), :]
                    total = term if total is None else total + term
                summed.append(total)
            for ey in range(6):
                if (ex, ey) not in around:
                    continue
                at = pl.ds(6 * ex + ey, 1)
                value = None
                if 1 <= ey <= 4:
                    value = YF[6 + ey] * summed[0]
                if 1 <= ex <= 4:
                    term = YF[ey] * summed[1]
                    value = term if value is None else value + term
                TR[0, at, :] = jnp.sum(value, axis=0, keepdims=True)
                if 1 <= ex <= 4 and 1 <= ey <= 4:
                    TR[1, at, :] = jnp.sum(YF[6 + ey] * summed[2], axis=0, keepdims=True)
        last = zop(TR[1], 3)
        grid = {}
        for tile in range(5):
            v = TR[0, pl.ds(8 * tile, 8), :] * imz
            v = v + j7 * pltpu.roll(v, 127, 1) + j0 * pltpu.roll(v, 1, 1)
            v = v + last[8 * tile : 8 * tile + 8]
            for k in range(8):
                if (8 * tile + k) // 6 < 6 and divmod(8 * tile + k, 6) in around:
                    grid[divmod(8 * tile + k, 6)] = v[k : k + 1]
        return share(grid)

    def with_sums(row, values):
        lanes = lane[0:1]
        for k, value in enumerate(values):
            row = row + jnp.where(lanes == 96 + k, value, zero)
        return row

    ga = ag_start(0, restricted_early())
    pend_g = list(ga)
    channels([3])
    warm = faces(L4, 1, 4, *set1, 6, start=768)
    pending += warm

    xsets = [(0, 1), (1,), (1, 2), (2,), (2, 3)]
    xclass = [0] + [1] * 6 + [2, 2] + [3] * 6 + [4]

    def spread(grid):
        planes = []
        for members in xsets:
            e = []
            for ey in range(4):
                total = grid[members[0]][ey]
                for ex in members[1:]:
                    total = total + grid[ex][ey]
                e.append(jnp.broadcast_to(total, (8, 128)))
            low = e[1] + s0 * e[0] + s7 * e[2]
            high = e[2] + s0 * e[1] + s7 * e[3]
            planes.append(zjoin(jnp.concatenate([low, high], 0)))
        return planes

    kplanes = spread(kgrid)
    mult = one / imyz
    for x in range(16):
        wa = jnp.float32(WTS[x % 8])
        ka = jnp.float32(KLN[x % 8])
        diag = (ka * cp[0] + wa * cp[3]) * kplanes[xclass[x]] + (
            jnp.float32(sigma_p) * wa / imx[x]
        ) * cp[0] * mult
        INVD[rows(x), :] = one / diag

    def coarse_planes(a):
        lanes = lane[0:1]
        accs = [None] * 9
        for z in range(nz):
            own = ag3[a, z]
            first, second = own[0:1], own[1:2]
            if z > 0:
                first = first + jnp.where(lanes < 32, ag3[a, z - 1][2:3], zero)
            if z < nz - 1:
                second = second + jnp.where(lanes >= 96, ag3[a, z + 1][2:3], zero)
            for h, part in enumerate((first, second)):
                wide = jnp.broadcast_to(part, (4, 128))
                for n in range(9):
                    term = CX[n, :, pl.ds((2 * z + h) * 128, 128)] * wide
                    accs[n] = term if accs[n] is None else accs[n] + term
        values = [jnp.sum(acc, axis=1, keepdims=True) for acc in accs]
        grid = []
        for ex in range(4):
            line = []
            for ey in range(4):
                dx, dy, _ = where_from(ex + 1, ey + 1)
                value = values[slot_of(dx, dy)]
                line.append(jnp.sum(OH[6 * ex + ey + 7] * value, axis=0, keepdims=True))
            grid.append(line)
        planes = [plane * imyz for plane in spread(grid)]
        return [imx[0] * planes[0], planes[1], half * planes[2], planes[3], imx[15] * planes[4]]

    def apply_local(q, put):
        T3[...] = zop(q[...], 2)
        for ex in range(2):
            planes = [q[rows(8 * ex + a), :] for a in range(8)]
            stiff = xop(planes, STF, 1)
            kap = KAP[pl.ds(16 * ex, 16), :]
            for i in range(8):
                x = 8 * ex + i
                wa = jnp.float32(WTS[i])
                kx = stiff[i]
                ky = yop(planes[i], 2)
                inner = cp[0] * kx + wa * (cp[1] * ky + cp[2] * T3[rows(x), :])
                put(x, planes[i], kap * inner + (jnp.float32(sigma_p) * wa) * (cp[0] * planes[i]))

    def apply_coarse(values):
        flat_z = zop(jnp.concatenate(values, 0), 2)
        rest = [
            cp[1] * yop(values[k], 2) + cp[2] * flat_z[16 * k : 16 * k + 16] for k in range(5)
        ]
        scaled = [cp[0] * values[k] for k in range(5)]
        out = []
        for ex in range(2):
            kap = KAP[pl.ds(16 * ex, 16), :]
            low, mid, high = scaled[2 * ex], scaled[2 * ex + 1], scaled[2 * ex + 2]
            for i in range(8):
                wa = jnp.float32(WTS[i])
                k = xclass[8 * ex + i]
                kx = (
                    jnp.float32(STF[i, 0]) * low
                    + jnp.float32(np.sum(STF[i, 1:7])) * mid
                    + jnp.float32(STF[i, 7]) * high
                )
                out.append(kap * (kx + wa * rest[k]) + (jnp.float32(sigma_p) * wa) * scaled[k])
        return out

    def put_joined(x, plane, value):
        L1[rows(x), :] = zjoin(value)

    upper = SBOUND
    lower = cheb_ratio * upper
    theta = 0.5 * (upper + lower)
    delta = 0.5 * (upper - lower)
    rho = delta / theta
    rho_next = 1.0 / (2.0 * theta / delta - rho)
    c2 = 2.0 * rho_next / delta
    c1 = jnp.float32((1.0 + rho_next * rho) / theta + c2)
    c2 = jnp.float32(c2 / theta)

    def renew(channels):
        for x in range(16):
            scale = (jnp.float32(dt_step / WTS[x % 8]) * imx[x]) * (imyz * cp[4])
            for c in channels:
                at = rows(x, 256 * c)
                FN[at, :] = F[at, :] + L4[at, :] * scale

    finish(now, L4, 3, 1, rx4, ry4, rc4)
    renew(range(3))
    T3[...] = zop(FN[pl.ds(512, 256), :], 0)
    for ex in range(2):
        slopes = xop([FN[rows(8 * ex + a), :] for a in range(8)], DER, -1)
        for i in range(8):
            x = 8 * ex + i
            div = slopes[i] + yop(FN[rows(x, 256), :], 0) + T3[rows(x), :]
            L1[rows(x), :] = zjoin(-(W[rows(x), :] * div))
    xyjoin(L1)

    now = faces(L1, 1, 0, *set1, 2)
    pending += now
    ga = ag_second(0, ga)
    pend_g += ga
    finish(now, L1, 1, 0, rx1, ry1, rc1)
    R0[...] = L1[...]
    T1[...] = L1[...] * INVD[...]
    apply_local(T1, put_joined)
    xyjoin(L1)
    now = faces(L1, 1, 1, *set1, 3)
    pending += now
    finish(warm, L4, 1, 4, rx1, ry1, rc1, start=768)
    renew([3])
    store_f = pltpu.make_async_copy(FN, out_f, l_sem.at[13])
    store_f.start()
    finish(now, L1, 1, 1, rx1, ry1, rc1)
    S0[...] = c1 * T1[...] - c2 * (INVD[...] * L1[...])

    def put_smooth(x, plane, value):
        W1[rows(x), :] = value

    apply_local(S0, put_smooth)
    for copy in rowsc:
        copy.wait_recv()
    ag_end(0, ga)
    values = coarse_planes(0)

    images = apply_coarse(values)
    dot = rz_part = None
    for x in range(16):
        at = rows(x)
        z0 = S0[at, :] + values[xclass[x]]
        value = W1[at, :] + images[x]
        Z0[at, :] = z0
        W1[at, :] = value
        L1[at, :] = zjoin(value)
        term = z0 * value
        dot = term if dot is None else dot + term
        term = imx[x] * (R0[at, :] * z0)
        rz_part = term if rz_part is None else rz_part + term

    def full(v):
        return jnp.sum(jnp.sum(v, axis=0, keepdims=True), axis=1, keepdims=True)

    xyjoin(L1)
    row = with_sums(restricted(L1), [full(rz_part * imyz), full(dot)])
    ga = ag_start(1, row)
    pend_g += ga
    now = faces(L1, 1, 2, *set1, 4)
    pending += now
    finish(now, L1, 1, 2, rx1, ry1, rc1)
    T2[...] = L1[...]
    T1[...] = L1[...] * INVD[...]
    apply_local(T1, put_joined)
    xyjoin(L1)
    now = faces(L1, 1, 3, *set1, 5)
    pending += now
    ga = ag_second(1, ga)
    pend_g += ga
    finish(now, L1, 1, 3, rx1, ry1, rc1)
    ZI[...] = c1 * T1[...] - c2 * (INVD[...] * L1[...])

    def put_second(x, plane, value):
        W2[rows(x), :] = value

    apply_local(ZI, put_second)
    ag_end(1, ga)
    rz0, curv0 = sums(1, 2)
    step0 = rz0 / curv0
    values = coarse_planes(1)

    images = apply_coarse(values)
    rz_part = None
    dots = [None, None]
    for x in range(16):
        at = rows(x)
        z0 = Z0[at, :]
        first = W1[at, :]
        z1 = z0 - step0 * (ZI[at, :] + values[xclass[x]])
        second = first - step0 * (W2[at, :] + images[x])
        ZI[at, :] = z1
        term = imx[x] * ((R0[at, :] - step0 * T2[at, :]) * z1)
        rz_part = term if rz_part is None else rz_part + term
        terms = (z1 * second, z0 * second + z1 * first)
        for k in range(2):
            dots[k] = terms[k] if dots[k] is None else dots[k] + terms[k]

    row = with_sums(
        jnp.zeros((1, 128), F32), [full(rz_part * imyz), full(dots[0]), full(dots[1])]
    )
    ga = ag_start(2, row)
    for copy in pending + side + rowsc + pend_g:
        copy.wait_send()
    store_f.wait()
    for copy in ga:
        copy.wait_send()
    ga = ag_second(2, ga, True)
    for copy in ga:
        copy.wait_send()
    ag_end(2, ga)
    rz1, a11, a10 = sums(2, 3)
    beta = rz1 / rz0
    curv1 = a11 + beta * a10 + beta * beta * curv0
    step1 = rz1 / curv1
    PC[...] = (step0 + step1 * beta) * Z0[...] + step1 * ZI[...]
    store_p = pltpu.make_async_copy(PC, out_p, l_sem.at[14])
    store_p.start()

    store_p.wait()


def per_device(nx, ny, nxc, fields, viscosity, inv_density, elem_group, coarse_inverse):
    nz = nx // nxc
    cy, bz, cp, spr, fy = constants()
    coarse = coarse_inverse
    if nxc * ny != XC * YL:
        coarse = coarse.reshape(NCD, nz, nxc, ny, NCD)
        coarse = jnp.pad(coarse, ((0, 0), (0, 0), (0, XC - nxc), (0, YL - ny), (0, 0)))
        coarse = coarse.reshape(NCD, nz * XC * YL * NCD)
    ncp = coarse.shape[1]

    def vm(*shape):
        return pltpu.VMEM(shape, F32)

    field = vm(256, 128)
    scratch = [
        vm(2, 2, 16), pltpu.VMEM((2, 2, 16), jnp.int32), vm(3, 8, 8, 128),
        pltpu.VMEM((4, 256, 256), BF16), vm(5, 16, 128), vm(16, 128), vm(36, 16, 128),
        vm(12, 16, 128), vm(1024, 128), vm(2, 40, 128),
        vm(1024, 128), vm(1024, 128), vm(1024, 128), vm(1024, 128), field,
        vm(1024, 128), vm(1024, 128), field, vm(1024, 128), field, field, field,
        vm(32, 128), field, vm(9, NCD, ncp), vm(8, 128), vm(8, 8, 128), vm(36, 4, 128), field,
        field, field, field, field, field, field, field, field,
        vm(2, 2, 64, 128), vm(2, 2, 64, 128), vm(2, 4, 4, 128),
        vm(2, 2, 64, 128), vm(2, 2, 64, 128), vm(2, 4, 4, 128),
        vm(5, 2, 16, 128), vm(5, 2, 16, 128), vm(5, 4, 1, 128),
        vm(5, 2, 16, 128), vm(5, 2, 16, 128), vm(5, 4, 1, 128),
        vm(3, nxc, ny, 1, 128), vm(3, nz, 4, 128),
        pltpu.SemaphoreType.DMA((7, 8)), pltpu.SemaphoreType.DMA((7, 8)),
        pltpu.SemaphoreType.DMA((8,)), pltpu.SemaphoreType.DMA((8,)),
        pltpu.SemaphoreType.DMA((8,)), pltpu.SemaphoreType.DMA((8,)),
        pltpu.SemaphoreType.DMA((3, 76)), pltpu.SemaphoreType.DMA((3, 76)),
        pltpu.SemaphoreType.DMA((15,)),
    ]
    anywhere = pl.BlockSpec(memory_space=pl.ANY)
    new, pressure = pl.pallas_call(
        functools.partial(kernel, nx, ny, nxc),
        out_shape=(
            jax.ShapeDtypeStruct((1024, 128), F32),
            jax.ShapeDtypeStruct((256, 128), F32),
        ),
        in_specs=[pl.BlockSpec(memory_space=pltpu.HBM)] * 10,
        out_specs=(anywhere, anywhere),
        scratch_shapes=scratch,
        compiler_params=pltpu.CompilerParams(
            collective_id=0, has_side_effects=True, vmem_limit_bytes=24 << 20
        ),
    )(
        *[pltpu.with_memory_space_constraint(v, pltpu.HBM) for v in (
        fields.reshape(1024, 128),
        viscosity.reshape(256, 128),
        inv_density,
        elem_group,
        coarse,
        cy, bz, cp, spr, fy)],
    )
    return new.reshape(fields.shape), pressure.reshape(viscosity.shape)


def build(mesh, nxc):
    placed = (
        P(None, "gx", None, "gy", None, None),
        P("gx", None, "gy", None, None),
        P("gx", "gy", None),
        P("gx", "gy", None),
        P(("gx", "gy"), None),
    )
    return jax.shard_map(
        functools.partial(per_device, mesh.shape["gx"], mesh.shape["gy"], nxc),
        mesh=mesh,
        in_specs=placed,
        out_specs=(P(None, "gx", None, "gy", None, None), P("gx", None, "gy", None, None)),
        check_vma=False,
    )


def solution(mesh):
    return build(mesh, XC)
```

```python
import functools

import jax
import jax.numpy as jnp
import numpy as np
from jax import lax
from jax.experimental import pallas as pl
from jax.experimental.pallas import tpu as pltpu
from jax.sharding import PartitionSpec as P

NCD = 4
XC = 8
YL = 8

dt_step = 0.01
sigma_p = 4.0
prandtl = 0.7
cheb_ratio = 0.1

F32 = jnp.float32
BF16 = jnp.bfloat16
DIRS = [(-1, 0), (1, 0), (0, -1), (0, 1), (-1, -1), (-1, 1), (1, -1), (1, 1)]
MESH = pl.DeviceIdType.MESH


def tables():
    points = np.array(
        [
            -1.0,
            -0.8717401485096066,
            -0.5917001814331423,
            -0.2092992179024789,
            0.2092992179024789,
            0.5917001814331423,
            0.8717401485096066,
            1.0,
        ]
    )
    weights = np.array(
        [
            1.0 / 28.0,
            0.2107042271435061,
            0.3411226924835044,
            0.4124587946587038,
            0.4124587946587038,
            0.3411226924835044,
            0.2107042271435061,
            1.0 / 28.0,
        ]
    )
    identity = np.eye(8)
    differ = points[:, None] - points[None, :] + identity
    barycentric = 1.0 / np.prod(differ, axis=1)
    offdiag = barycentric[None, :] / barycentric[:, None] / differ * (1.0 - identity)
    derivative = offdiag - identity * np.sum(offdiag, axis=1)[:, None]
    mass_one = identity * weights[None, :]
    stiff_one = derivative.T @ mass_one @ derivative
    stiff_three = (
        np.kron(np.kron(stiff_one, mass_one), mass_one)
        + np.kron(np.kron(mass_one, stiff_one), mass_one)
        + np.kron(np.kron(mass_one, mass_one), stiff_one)
    )
    three_diag = np.sum(stiff_three * np.eye(512), axis=1)
    spectral_bound = float(np.max(np.sum(np.abs(stiff_three), axis=1) / three_diag))
    return derivative, weights, stiff_one, spectral_bound


DER, WTS, STF, SBOUND = tables()
KLN = np.diag(STF)


def functionals():
    count = 8
    found = []
    for first in (3, 0, count - 2):
        both = np.zeros((2, 6, 16))
        mult = np.ones((count, 8))
        mult[1:, 0] = 2.0
        mult[:-1, 7] = 2.0
        for place in range(6):
            e = first - 2 + place
            if not 0 <= e < count:
                continue
            phi = np.zeros((count, 8))
            phi[e] = 1.0 / mult[e]
            if e > 0:
                phi[e - 1, 7] = phi[e, 0]
            if e < count - 1:
                phi[e + 1, 0] = phi[e, 7]
            t = -(phi * WTS[None, :]) @ DER
            joint = t[:-1, 7] + t[1:, 0]
            t[:-1, 7] = joint
            t[1:, 0] = joint
            t = t / (mult * WTS[None, :])
            both[0, place] = t[first : first + 2].reshape(16)
            both[1, place] = phi[first : first + 2].reshape(16)
        found.append(both)
    return np.stack(found, 0)


def z_functional():
    mult = np.ones((16, 8))
    mult[1:, 0] = 2.0
    mult[:-1, 7] = 2.0
    full = np.zeros((128, 128))
    for e in range(16):
        phi = np.zeros((16, 8))
        phi[e] = 1.0 / mult[e]
        if e > 0:
            phi[e - 1, 7] = phi[e, 0]
        if e < 15:
            phi[e + 1, 0] = phi[e, 7]
        t = -(phi * WTS[None, :]) @ DER
        joint = t[:-1, 7] + t[1:, 0]
        t[:-1, 7] = joint
        t[1:, 0] = joint
        t = t / (mult * WTS[None, :])
        full[:, 8 * e : 8 * e + 8] = t.reshape(128)[:, None] / 8.0
    return full


FUN = functionals()


def constants():
    cols = np.stack([DER, DER.T, STF], 0)
    cy = np.broadcast_to(np.transpose(cols, (0, 2, 1))[:, :, :, None], (3, 8, 8, 128))

    def big(one):
        full = (one if one.shape[0] == 128 else np.kron(np.eye(16), one)).astype(np.float32)
        high = np.asarray(full, dtype=jnp.bfloat16)
        low = np.asarray(full - high.astype(np.float32), dtype=jnp.bfloat16)
        return np.block([[high, low], [high, np.zeros_like(low)]])

    bz = np.stack([big(DER.T), big(DER), big(STF), big(z_functional())], 0)
    wy = np.tile(WTS, 2)[:, None]
    ky = np.tile(KLN, 2)[:, None]
    wz = np.tile(WTS, 16)[None, :]
    kz = np.tile(KLN, 16)[None, :]
    one = np.ones((16, 128))
    cp = np.stack([wy * wz, one * wz, wy * one, ky * wz + wy * kz, 1.0 / (wy * wz)], 0)
    spread = np.kron(np.eye(16), np.ones((1, 8)))
    fy = np.stack([FUN[0], FUN[1] - FUN[0], FUN[2] - FUN[0]], 0).reshape(36, 16)
    fy = np.broadcast_to(fy[:, :, None], (36, 16, 128))
    return (
        jnp.asarray(np.ascontiguousarray(cy), F32),
        jnp.asarray(bz, BF16),
        jnp.asarray(cp, F32),
        jnp.asarray(spread, F32),
        jnp.asarray(np.ascontiguousarray(fy), F32),
    )


def kernel(
    nx, ny, nxc,
    fields, visc, dens_h, grp_h, coarse, cy_h, bz_h, cp_h, spr_h, fy_h,
    out_f, out_p,
    dens, grp, cy, bz, cp, spr, fy, YF, G, TR, C1, C2, C3, C4, W2,
    F, FN, V, L4, L1, W, IM, KAP, INVD, CX, AUX, AUXR, OH, PC,
    T1, T2, T3, R0, S0, Z0, W1, ZI,
    sx4, sy4, sc4, rx4, ry4, rc4, sx1, sy1, sc1, rx1, ry1, rc1,
    ag1, ag3,
    s_sem, r_sem, as_sem, ar_sem, cs_sem, cr_sem, gs_sem, gr_sem, l_sem,
):
    gx = lax.axis_index("gx")
    gy = lax.axis_index("gy")
    nz = nx // nxc
    xc = gx % nxc
    zc = gx // nxc

    def nbr(dx, dy):
        return ((gx + dx + nx) % nx, (gy + dy + ny) % ny)

    def z_mate(k):
        return (((zc + k) % nz) * nxc + xc, gy)

    def hops(off):
        dx, dy = off
        chips = dx // 2
        return min(chips, nxc // 2 - chips) + min(dy, ny - dy)

    flat = [(dx, dy) for dx in range(nxc) for dy in range(ny)][1:]
    flat.sort(key=hops, reverse=True)
    zline = sorted(range(1, nz), key=lambda k: -min(k, nz - k))

    def p_mate(dx, dy):
        return (zc * nxc + (xc + dx) % nxc, (gy + dy) % ny)

    load_f = []
    for c in range(4):
        part = pl.ds(256 * c, 256)
        load_f.append(pltpu.make_async_copy(fields.at[part], F.at[part], l_sem.at[c]))
    small = [(dens_h, dens), (grp_h, grp), (spr_h, spr), (cp_h, cp)]
    large = [(cy_h, cy), (bz_h, bz), (visc, V), (fy_h, fy)]
    load_s = [
        pltpu.make_async_copy(src, dst, l_sem.at[4 + k]) for k, (src, dst) in enumerate(small)
    ]
    load_l = [
        pltpu.make_async_copy(src, dst, l_sem.at[8 + k]) for k, (src, dst) in enumerate(large)
    ]
    load_c = pltpu.make_async_copy(coarse, CX.at[8], l_sem.at[12])
    for copy in load_f + load_s + load_l + [load_c]:
        copy.start()

    ranked = [(hops(off), p_mate(*off)) for off in flat]
    ranked += [(min(k, nz - k), z_mate(k)) for k in zline]
    ranked += [(2 + abs(dy), nbr(dx, dy)) for dx, dy in DIRS if dx != 0 or nxc * ny < 4]
    ranked.sort(key=lambda item: -item[0])
    mates = [mate for _, mate in ranked]
    barrier = pltpu.get_barrier_semaphore()
    for mate in mates:
        pl.semaphore_signal(barrier, inc=1, device_id=mate, device_id_type=MESH)

    lane = lax.broadcasted_iota(jnp.int32, (8, 128), 1)
    sub = lax.broadcasted_iota(jnp.int32, (8, 128), 0)
    one = jnp.float32(1.0)
    zero = jnp.float32(0.0)
    j7 = jnp.where((lane % 8 == 7) & (lane < 127), one, zero)
    j0 = jnp.where((lane % 8 == 0) & (lane > 0), one, zero)
    j7p = jnp.concatenate([j7, j7], 0)
    j0p = jnp.concatenate([j0, j0], 0)
    s0 = jnp.where(sub == 0, one, zero)
    s7 = jnp.where(sub == 7, one, zero)

    has_l = jnp.where(gx > 0, one, zero)
    has_r = jnp.where(gx < nx - 1, one, zero)
    has_b = jnp.where(gy > 0, one, zero)
    has_t = jnp.where(gy < ny - 1, one, zero)
    vx = {-1: has_l, 0: one, 1: has_r}
    vy = {-1: has_b, 0: one, 1: has_t}

    def zjoin(v):
        return v + j7p * pltpu.roll(v, 127, 1) + j0p * pltpu.roll(v, 1, 1)

    def rows(x, base=0):
        return pl.ds(base + 16 * x, 16)

    def xyjoin(L, base=0):
        both = L[pl.ds(base + 112, 16), :] + L[pl.ds(base + 128, 16), :]
        L[pl.ds(base + 112, 16), :] = both
        L[pl.ds(base + 128, 16), :] = both
        pair = L[pl.ds(base + 7, 16, stride=16), :] + L[pl.ds(base + 8, 16, stride=16), :]
        L[pl.ds(base + 7, 16, stride=16), :] = pair
        L[pl.ds(base + 8, 16, stride=16), :] = pair

    def yop(plane, which):
        parts = []
        for t in range(2):
            tile = plane[8 * t : 8 * t + 8, :]
            total = None
            for b in range(8):
                term = jnp.broadcast_to(tile[b : b + 1, :], (8, 128)) * cy[which, b]
                total = term if total is None else total + term
            parts.append(total)
        return jnp.concatenate(parts, 0)

    def xop(planes, matrix, sign):
        even = [planes[a] + planes[7 - a] for a in range(4)]
        odd = [planes[a] - planes[7 - a] for a in range(4)]
        out = [None] * 8
        for i in range(4):
            p = q = None
            for a in range(4):
                both = even[a] * jnp.float32((matrix[i, a] + matrix[i, 7 - a]) / 2)
                diff = odd[a] * jnp.float32((matrix[i, a] - matrix[i, 7 - a]) / 2)
                p = both if p is None else p + both
                q = diff if q is None else q + diff
            out[i] = p + q
            out[7 - i] = p - q if sign > 0 else q - p
        return out

    def zop(f, which):
        high = f.astype(BF16)
        low = (f - high.astype(F32)).astype(BF16)
        both = jnp.concatenate([high, low], 1)
        prod = jnp.dot(both, bz[which], preferred_element_type=F32)
        return prod[:, :128] + prod[:, 128:]

    def faces(L, nch, e, sx, sy, sc, rx, ry, rc, num, start=0):
        used = pl.ds(0, 16 * nch)
        for c in range(nch):
            base = start + 256 * c
            sx[e, 0, pl.ds(16 * c, 16), :] = L[pl.ds(base, 16), :]
            sx[e, 1, pl.ds(16 * c, 16), :] = L[pl.ds(base + 240, 16), :]
            sy[e, 0, pl.ds(16 * c, 16), :] = L[pl.ds(base, 16, stride=16), :]
            sy[e, 1, pl.ds(16 * c, 16), :] = L[pl.ds(base + 15, 16, stride=16), :]
            for k, (dx, dy) in enumerate(DIRS[4:]):
                row = base + (240 if dx > 0 else 0) + (15 if dy > 0 else 0)
                sc[e, k, pl.ds(c, 1), :] = L[pl.ds(row, 1), :]
        copies = []
        for d in (4, 5, 6, 7, 0, 1, 2, 3):
            if d < 2:
                src, dst = sx.at[e, d, used], rx.at[e, d, used]
            elif d < 4:
                src, dst = sy.at[e, d - 2, used], ry.at[e, d - 2, used]
            else:
                src, dst = sc.at[e, d - 4], rc.at[e, d - 4]
            copy = pltpu.make_async_remote_copy(
                src, dst, s_sem.at[num, d], r_sem.at[num, d],
                device_id=nbr(*DIRS[d]), device_id_type=MESH,
            )
            copy.start()
            copies.append(copy)
        return copies

    def finish(copies, L, nch, e, rx, ry, rc, start=0):
        for copy in copies:
            copy.wait_recv()
        for c in range(nch):
            base = start + 256 * c
            at = pl.ds(16 * c, 16)
            lo, hi = pl.ds(base, 16), pl.ds(base + 240, 16)
            L[lo, :] = L[lo, :] + has_l * rx[e, 1, at, :]
            L[hi, :] = L[hi, :] + has_r * rx[e, 0, at, :]
            lo, hi = pl.ds(base, 16, stride=16), pl.ds(base + 15, 16, stride=16)
            L[lo, :] = L[lo, :] + has_b * ry[e, 1, at, :]
            L[hi, :] = L[hi, :] + has_t * ry[e, 0, at, :]
            for k, (dx, dy) in enumerate(DIRS[4:]):
                row = pl.ds(base + (0 if dx > 0 else 240) + (0 if dy > 0 else 15), 1)
                L[row, :] = L[row, :] + (vx[-dx] * vy[-dy]) * rc[e, k, pl.ds(c, 1), :]

    set4 = (sx4, sy4, sc4, rx4, ry4, rc4)
    set1 = (sx1, sy1, sc1, rx1, ry1, rc1)
    pending = []

    def joined(c):
        load_f[c].wait()
        for x in range(16):
            L4[rows(x, 256 * c), :] = zjoin(F[rows(x, 256 * c), :])
        xyjoin(L4, 256 * c)

    for c in range(3):
        joined(c)
    for e in range(2):
        for k in range(4):
            sc4[e, k, pl.ds(3, 1), :] = jnp.zeros((1, 128), F32)
    pl.semaphore_wait(barrier, len(mates))
    now = faces(L4, 3, 0, *set4, 0)
    pending += now
    joined(3)
    heat = faces(L4, 1, 5, *set1, 7, start=768)
    pending += heat
    for copy in load_s:
        copy.wait()
    for ex in range(2):
        AUX[pl.ds(2 * ex, 2), :] = jnp.dot(
            dens[ex], spr[...], preferred_element_type=F32, precision=lax.Precision.HIGHEST
        )
        AUX[pl.ds(4 + 2 * ex, 2), :] = jnp.dot(
            grp[ex].astype(F32), spr[...], preferred_element_type=F32,
            precision=lax.Precision.HIGHEST,
        )
    for ex in range(2):
        for ey in range(2):
            row = AUX[pl.ds(2 * ex + ey, 1), :]
            KAP[pl.ds(16 * ex + 8 * ey, 8), :] = jnp.broadcast_to(row, (8, 128))

    side = []
    for d, (dx, dy) in enumerate(DIRS):
        copy = pltpu.make_async_remote_copy(
            AUX, AUXR.at[d], as_sem.at[d], ar_sem.at[d],
            device_id=nbr(dx, dy), device_id_type=MESH,
        )
        copy.start()
        side.append(copy)
    rowsc = []
    for d, (dx, dy) in enumerate(DIRS):
        copy = pltpu.make_async_remote_copy(
            coarse, CX.at[d], cs_sem.at[d], cr_sem.at[d],
            device_id=nbr(dx, dy), device_id_type=MESH,
        )
        copy.start()
        rowsc.append(copy)

    half = jnp.float32(0.5)
    imx = [one] * 16
    imx[0] = jnp.where(gx > 0, half, one)
    imx[7] = imx[8] = half
    imx[15] = jnp.where(gx < nx - 1, half, one)
    imz = one - half * (j7 + j0)
    imy0 = one - half * s7 - (half * has_b) * s0
    imy1 = one - half * s0 - (half * has_t) * s7
    imyz = jnp.concatenate([imy0 * imz, imy1 * imz], 0)
    for x in range(16):
        W[rows(x), :] = jnp.float32(WTS[x % 8]) * cp[0]
        IM[rows(x), :] = imx[x] * imyz

    for copy in load_l + [load_c]:
        copy.wait()
    V[...] = V[...] * W[...]
    no_b, no_t = one - has_b, one - has_t
    for k in range(12):
        YF[k] = fy[k] + no_b * fy[12 + k] + no_t * fy[24 + k]
    finish(now, L4, 3, 0, rx4, ry4, rc4)
    for c in range(3):
        at = pl.ds(256 * c, 256)
        F[at, :] = L4[at, :] * IM[...]

    for copy in side:
        copy.wait_recv()

    def where_from(ex, ey):
        return ex // 2 - 1, ey // 2 - 1, 2 * (ex % 2) + ey % 2

    def slot_of(dx, dy):
        return 8 if (dx, dy) == (0, 0) else DIRS.index((-dx, -dy))

    around = [
        (ex, ey) for ex in range(6) for ey in range(6) if not (ex in (0, 5) and ey in (0, 5))
    ]
    kgrid = [[None] * 4 for _ in range(4)]
    for ex, ey in around:
        dx, dy, local = where_from(ex, ey)
        slot = slot_of(dx, dy)
        valid = vx[dx] * vy[dy]
        if slot == 8:
            krow = AUX[pl.ds(local, 1), :]
            grow = AUX[pl.ds(4 + local, 1), :]
        else:
            krow = AUXR[slot, pl.ds(local, 1), :]
            grow = AUXR[slot, pl.ds(4 + local, 1), :]
        if 1 <= ex <= 4 and 1 <= ey <= 4:
            kgrid[ex - 1][ey - 1] = krow * valid
        hit = jnp.abs(jnp.broadcast_to(grow, (4, 128)) - sub[0:4].astype(F32)) < half
        OH[6 * ex + ey] = jnp.where(hit, valid, zero)

    def channels(which):
        for c in which:
            at = pl.ds(256 * c, 256)
            C3[at, :] = zop(F[at, :], 0)
        for c in which:
            base = 256 * c
            coef = None if c < 3 else jnp.float32(1.0 / prandtl)
            for ex in range(2):
                planes = [F[rows(8 * ex + a, base), :] for a in range(8)]
                slopes = xop(planes, DER, -1)
                for i in range(8):
                    x = 8 * ex + i
                    gxp = slopes[i]
                    gyp = yop(planes[i], 0)
                    gzp = C3[rows(x, base), :]
                    adv = (
                        F[rows(x), :] * gxp + F[rows(x, 256), :] * gyp + F[rows(x, 512), :] * gzp
                    )
                    nuw = V[rows(x), :] if coef is None else coef * V[rows(x), :]
                    C1[rows(x, base), :] = nuw * gxp
                    C2[rows(x, base), :] = yop(nuw * gyp, 1) + W[rows(x), :] * adv
                    C4[rows(x, base), :] = nuw * gzp
            at = pl.ds(base, 256)
            C3[at, :] = zop(C4[at, :], 1)
        for c in which:
            base = 256 * c
            for ex in range(2):
                turned = xop([C1[rows(8 * ex + a, base), :] for a in range(8)], DER.T, -1)
                for i in range(8):
                    x = 8 * ex + i
                    at = rows(x, base)
                    total = turned[i] + (C3[at, :] + C2[at, :])
                    if c < 3:
                        G[at, :] = W[rows(x), :] * F[at, :] - jnp.float32(dt_step) * total
                    L4[at, :] = zjoin(-total)
            xyjoin(L4, base)

    channels(range(3))
    now = faces(L4, 3, 1, *set4, 1)
    pending += now

    group = lane[0:1] // 32
    parts = [jnp.where(group == g, one, zero) for g in range(4)]

    def ag_start(a, row):
        ag1[a, xc, 0] = row
        out = []
        for dx, dy in flat:
            copy = pltpu.make_async_remote_copy(
                ag1.at[a, xc, 0], ag1.at[a, xc, dy],
                gs_sem.at[a, dx * ny + dy], gr_sem.at[a, dx * ny + dy],
                device_id=p_mate(dx, dy), device_id_type=MESH,
            )
            copy.start()
            out.append(copy)
        return out

    def ag_second(a, copies, only_sums=False):
        for copy in copies:
            copy.wait_recv()
        pre = [[None] * 3 for _ in range(4)]
        for xs in range(nxc):
            row = ag1[a, xs, 0]
            for k in range(1, ny):
                row = row + ag1[a, xs, k]
            for g in range(3, 4) if only_sums else range(4):
                t = xs + g - 1
                if g == 3:
                    row_at, to_at = 2, 1
                elif t < 0:
                    row_at, to_at = 2, 3
                elif t > nxc - 1:
                    row_at, to_at = 2, 0
                else:
                    row_at, to_at = t // 4, t % 4
                turn = (to_at - g) % 4
                part = row * parts[g]
                old = pre[turn][row_at]
                pre[turn][row_at] = part if old is None else old + part
        blank = jnp.zeros((1, 128), F32)
        message = None
        for turn in range(4):
            if all(row is None for row in pre[turn]):
                continue
            block = [blank if row is None else row for row in pre[turn]] + [blank] * 5
            block = jnp.concatenate(block, 0)
            if turn:
                block = pltpu.roll(block, 32 * turn, 1)
            message = block if message is None else message + block
        ag3[a, zc] = message[0:4]
        out = []
        for k in zline:
            copy = pltpu.make_async_remote_copy(
                ag3.at[a, zc], ag3.at[a, zc], gs_sem.at[a, 64 + k], gr_sem.at[a, 64 + k],
                device_id=z_mate(k), device_id_type=MESH,
            )
            copy.start()
            out.append(copy)
        return out

    def ag_end(a, copies):
        for copy in copies:
            copy.wait_recv()

    def sums(a, count):
        total = ag3[a, 0][2:3]
        for z in range(1, nz):
            total = total + ag3[a, z][2:3]
        lanes = lane[0:1]
        return [
            jnp.sum(jnp.where(lanes == 32 + k, total, zero), axis=1, keepdims=True)
            for k in range(count)
        ]

    devs = [(dx, dy) for dx in (-1, 0, 1) for dy in (-1, 0, 1)]
    members = {dev: [] for dev in devs}
    for ex, ey in around:
        dx, dy, _ = where_from(ex, ey)
        members[(dx, dy)].append((ex, ey))

    def restricted(L):
        x_first = imx[0] * L[rows(0), :]
        x_last = imx[15] * L[rows(15), :]
        low, high = x_first, x_last
        for x in range(1, 7):
            low = low + L[rows(x), :]
            high = high + L[rows(x + 8), :]
        low = low + half * L[rows(7), :]
        high = high + half * L[rows(8), :]
        grid = {}
        for ex, part in enumerate((x_first, low, high, x_last)):
            part = part * imyz
            t0, t1 = part[0:8], part[8:16]
            grid[ex + 1, 1] = t0[0:1]
            grid[ex + 1, 2] = jnp.sum(t0, axis=0, keepdims=True)
            grid[ex + 1, 3] = jnp.sum(t1, axis=0, keepdims=True)
            grid[ex + 1, 4] = t1[7:8]
        return share(grid)

    def share(grid):
        message = jnp.zeros((4, 128), F32)
        for dx, dy in devs:
            acc = None
            for ex, ey in members[(dx, dy)]:
                if (ex, ey) not in grid:
                    continue
                term = jnp.broadcast_to(grid[ex, ey], (4, 128)) * OH[6 * ex + ey]
                acc = term if acc is None else acc + term
            value = jnp.sum(acc, axis=1, keepdims=True)
            to = 32 * (dx + 1) + ((gy + dy + YL) % YL) * NCD + sub[0:4]
            message = message + jnp.where(lane[0:4] == to, value, zero)
        return jnp.sum(message, axis=0, keepdims=True)

    def along(table, ex, x):
        c0 = FUN[0, table, ex, x]
        cl, cr = FUN[1, table, ex, x] - c0, FUN[2, table, ex, x] - c0
        if max(abs(c0), abs(cl), abs(cr)) < 1e-12:
            return None
        value = jnp.float32(c0)
        if abs(cl) > 1e-12:
            value = value + jnp.float32(cl) * (one - has_l)
        if abs(cr) > 1e-12:
            value = value + jnp.float32(cr) * (one - has_r)
        return value

    def restricted_early():
        TR[...] = jnp.zeros((2, 40, 128), F32)
        for ex in range(6):
            summed = []
            for c, table in ((0, 0), (1, 1), (2, 1)):
                total = None
                for x in range(16):
                    coef = along(table, ex, x)
                    if coef is None:
                        continue
                    term = coef * G[rows(x, 256 * c), :]
                    total = term if total is None else total + term
                summed.append(total)
            for ey in range(6):
                if (ex, ey) not in around:
                    continue
                at = pl.ds(6 * ex + ey, 1)
                value = None
                if 1 <= ey <= 4:
                    value = YF[6 + ey] * summed[0]
                if 1 <= ex <= 4:
                    term = YF[ey] * summed[1]
                    value = term if value is None else value + term
                TR[0, at, :] = jnp.sum(value, axis=0, keepdims=True)
                if 1 <= ex <= 4 and 1 <= ey <= 4:
                    TR[1, at, :] = jnp.sum(YF[6 + ey] * summed[2], axis=0, keepdims=True)
        last = zop(TR[1], 3)
        grid = {}
        for tile in range(5):
            v = TR[0, pl.ds(8 * tile, 8), :] * imz
            v = v + j7 * pltpu.roll(v, 127, 1) + j0 * pltpu.roll(v, 1, 1)
            v = v + last[8 * tile : 8 * tile + 8]
            for k in range(8):
                if (8 * tile + k) // 6 < 6 and divmod(8 * tile + k, 6) in around:
                    grid[divmod(8 * tile + k, 6)] = v[k : k + 1]
        return share(grid)

    def with_sums(row, values):
        lanes = lane[0:1]
        for k, value in enumerate(values):
            row = row + jnp.where(lanes == 96 + k, value, zero)
        return row

    ga = ag_start(0, restricted_early())
    pend_g = list(ga)
    finish(heat, L4, 1, 5, rx1, ry1, rc1, start=768)
    F[pl.ds(768, 256), :] = L4[pl.ds(768, 256), :] * IM[...]
    channels([3])
    warm = faces(L4, 1, 4, *set1, 6, start=768)
    pending += warm

    xsets = [(0, 1), (1,), (1, 2), (2,), (2, 3)]
    xclass = [0] + [1] * 6 + [2, 2] + [3] * 6 + [4]

    def spread(grid):
        planes = []
        for members in xsets:
            e = []
            for ey in range(4):
                total = grid[members[0]][ey]
                for ex in members[1:]:
                    total = total + grid[ex][ey]
                e.append(jnp.broadcast_to(total, (8, 128)))
            low = e[1] + s0 * e[0] + s7 * e[2]
            high = e[2] + s0 * e[1] + s7 * e[3]
            planes.append(zjoin(jnp.concatenate([low, high], 0)))
        return planes

    kplanes = spread(kgrid)
    mult = one / imyz
    for x in range(16):
        wa = jnp.float32(WTS[x % 8])
        ka = jnp.float32(KLN[x % 8])
        diag = (ka * cp[0] + wa * cp[3]) * kplanes[xclass[x]] + (
            jnp.float32(sigma_p) * wa / imx[x]
        ) * cp[0] * mult
        INVD[rows(x), :] = one / diag

    def coarse_planes(a):
        lanes = lane[0:1]
        accs = [None] * 9
        for z in range(nz):
            own = ag3[a, z]
            first, second = own[0:1], own[1:2]
            if z > 0:
                first = first + jnp.where(lanes < 32, ag3[a, z - 1][2:3], zero)
            if z < nz - 1:
                second = second + jnp.where(lanes >= 96, ag3[a, z + 1][2:3], zero)
            for h, part in enumerate((first, second)):
                wide = jnp.broadcast_to(part, (4, 128))
                for n in range(9):
                    term = CX[n, :, pl.ds((2 * z + h) * 128, 128)] * wide
                    accs[n] = term if accs[n] is None else accs[n] + term
        values = [jnp.sum(acc, axis=1, keepdims=True) for acc in accs]
        grid = []
        for ex in range(4):
            line = []
            for ey in range(4):
                dx, dy, _ = where_from(ex + 1, ey + 1)
                value = values[slot_of(dx, dy)]
                line.append(jnp.sum(OH[6 * ex + ey + 7] * value, axis=0, keepdims=True))
            grid.append(line)
        planes = [plane * imyz for plane in spread(grid)]
        return [imx[0] * planes[0], planes[1], half * planes[2], planes[3], imx[15] * planes[4]]

    def apply_local(q, put):
        T3[...] = zop(q[...], 2)
        for ex in range(2):
            planes = [q[rows(8 * ex + a), :] for a in range(8)]
            stiff = xop(planes, STF, 1)
            kap = KAP[pl.ds(16 * ex, 16), :]
            for i in range(8):
                x = 8 * ex + i
                wa = jnp.float32(WTS[i])
                kx = stiff[i]
                ky = yop(planes[i], 2)
                inner = cp[0] * kx + wa * (cp[1] * ky + cp[2] * T3[rows(x), :])
                put(x, planes[i], kap * inner + (jnp.float32(sigma_p) * wa) * (cp[0] * planes[i]))

    def apply_coarse(values):
        flat_z = zop(jnp.concatenate(values, 0), 2)
        rest = [
            cp[1] * yop(values[k], 2) + cp[2] * flat_z[16 * k : 16 * k + 16] for k in range(5)
        ]
        scaled = [cp[0] * values[k] for k in range(5)]
        out = []
        for ex in range(2):
            kap = KAP[pl.ds(16 * ex, 16), :]
            low, mid, high = scaled[2 * ex], scaled[2 * ex + 1], scaled[2 * ex + 2]
            for i in range(8):
                wa = jnp.float32(WTS[i])
                k = xclass[8 * ex + i]
                kx = (
                    jnp.float32(STF[i, 0]) * low
                    + jnp.float32(np.sum(STF[i, 1:7])) * mid
                    + jnp.float32(STF[i, 7]) * high
                )
                out.append(kap * (kx + wa * rest[k]) + (jnp.float32(sigma_p) * wa) * scaled[k])
        return out

    def put_joined(x, plane, value):
        L1[rows(x), :] = zjoin(value)

    upper = SBOUND
    lower = cheb_ratio * upper
    theta = 0.5 * (upper + lower)
    delta = 0.5 * (upper - lower)
    rho = delta / theta
    rho_next = 1.0 / (2.0 * theta / delta - rho)
    c2 = 2.0 * rho_next / delta
    c1 = jnp.float32((1.0 + rho_next * rho) / theta + c2)
    c2 = jnp.float32(c2 / theta)

    def renew(channels):
        for x in range(16):
            scale = (jnp.float32(dt_step / WTS[x % 8]) * imx[x]) * (imyz * cp[4])
            for c in channels:
                at = rows(x, 256 * c)
                FN[at, :] = F[at, :] + L4[at, :] * scale

    finish(now, L4, 3, 1, rx4, ry4, rc4)
    renew(range(3))
    T3[...] = zop(FN[pl.ds(512, 256), :], 0)
    for ex in range(2):
        slopes = xop([FN[rows(8 * ex + a), :] for a in range(8)], DER, -1)
        for i in range(8):
            x = 8 * ex + i
            div = slopes[i] + yop(FN[rows(x, 256), :], 0) + T3[rows(x), :]
            L1[rows(x), :] = zjoin(-(W[rows(x), :] * div))
    xyjoin(L1)

    now = faces(L1, 1, 0, *set1, 2)
    pending += now
    ga = ag_second(0, ga)
    pend_g += ga
    finish(now, L1, 1, 0, rx1, ry1, rc1)
    R0[...] = L1[...]
    T1[...] = L1[...] * INVD[...]
    apply_local(T1, put_joined)
    xyjoin(L1)
    now = faces(L1, 1, 1, *set1, 3)
    pending += now
    finish(warm, L4, 1, 4, rx1, ry1, rc1, start=768)
    renew([3])
    store_f = pltpu.make_async_copy(FN, out_f, l_sem.at[13])
    store_f.start()
    finish(now, L1, 1, 1, rx1, ry1, rc1)
    S0[...] = c1 * T1[...] - c2 * (INVD[...] * L1[...])

    def put_smooth(x, plane, value):
        W1[rows(x), :] = value

    apply_local(S0, put_smooth)
    for copy in rowsc:
        copy.wait_recv()
    ag_end(0, ga)
    values = coarse_planes(0)

    images = apply_coarse(values)
    dot = rz_part = None
    for x in range(16):
        at = rows(x)
        z0 = S0[at, :] + values[xclass[x]]
        value = W1[at, :] + images[x]
        Z0[at, :] = z0
        W1[at, :] = value
        L1[at, :] = zjoin(value)
        term = z0 * value
        dot = term if dot is None else dot + term
        term = imx[x] * (R0[at, :] * z0)
        rz_part = term if rz_part is None else rz_part + term

    def full(v):
        return jnp.sum(jnp.sum(v, axis=0, keepdims=True), axis=1, keepdims=True)

    xyjoin(L1)
    row = with_sums(restricted(L1), [full(rz_part * imyz), full(dot)])
    ga = ag_start(1, row)
    pend_g += ga
    now = faces(L1, 1, 2, *set1, 4)
    pending += now
    finish(now, L1, 1, 2, rx1, ry1, rc1)
    T2[...] = L1[...]
    T1[...] = L1[...] * INVD[...]
    apply_local(T1, put_joined)
    xyjoin(L1)
    now = faces(L1, 1, 3, *set1, 5)
    pending += now
    ga = ag_second(1, ga)
    pend_g += ga
    finish(now, L1, 1, 3, rx1, ry1, rc1)
    ZI[...] = c1 * T1[...] - c2 * (INVD[...] * L1[...])

    def put_second(x, plane, value):
        W2[rows(x), :] = value

    apply_local(ZI, put_second)
    ag_end(1, ga)
    rz0, curv0 = sums(1, 2)
    step0 = rz0 / curv0
    values = coarse_planes(1)

    images = apply_coarse(values)
    rz_part = None
    dots = [None, None]
    for x in range(16):
        at = rows(x)
        z0 = Z0[at, :]
        first = W1[at, :]
        z1 = z0 - step0 * (ZI[at, :] + values[xclass[x]])
        second = first - step0 * (W2[at, :] + images[x])
        ZI[at, :] = z1
        term = imx[x] * ((R0[at, :] - step0 * T2[at, :]) * z1)
        rz_part = term if rz_part is None else rz_part + term
        terms = (z1 * second, z0 * second + z1 * first)
        for k in range(2):
            dots[k] = terms[k] if dots[k] is None else dots[k] + terms[k]

    row = with_sums(
        jnp.zeros((1, 128), F32), [full(rz_part * imyz), full(dots[0]), full(dots[1])]
    )
    ga = ag_start(2, row)
    for copy in pending + side + rowsc + pend_g:
        copy.wait_send()
    store_f.wait()
    for copy in ga:
        copy.wait_send()
    ga = ag_second(2, ga, True)
    for copy in ga:
        copy.wait_send()
    ag_end(2, ga)
    rz1, a11, a10 = sums(2, 3)
    beta = rz1 / rz0
    curv1 = a11 + beta * a10 + beta * beta * curv0
    step1 = rz1 / curv1
    PC[...] = (step0 + step1 * beta) * Z0[...] + step1 * ZI[...]
    store_p = pltpu.make_async_copy(PC, out_p, l_sem.at[14])
    store_p.start()

    store_p.wait()


def place(new, pressure, out_f, out_p, sems):
    first = pltpu.make_async_copy(new, out_f, sems.at[0])
    second = pltpu.make_async_copy(pressure, out_p, sems.at[1])
    first.start()
    second.start()
    first.wait()
    second.wait()


def per_device(nx, ny, nxc, fields, viscosity, inv_density, elem_group, coarse_inverse):
    nz = nx // nxc
    cy, bz, cp, spr, fy = constants()
    coarse = coarse_inverse
    if nxc * ny != XC * YL:
        coarse = coarse.reshape(NCD, nz, nxc, ny, NCD)
        coarse = jnp.pad(coarse, ((0, 0), (0, 0), (0, XC - nxc), (0, YL - ny), (0, 0)))
        coarse = coarse.reshape(NCD, nz * XC * YL * NCD)
    ncp = coarse.shape[1]

    def vm(*shape):
        return pltpu.VMEM(shape, F32)

    field = vm(256, 128)
    scratch = [
        vm(2, 2, 16), pltpu.VMEM((2, 2, 16), jnp.int32), vm(3, 8, 8, 128),
        pltpu.VMEM((4, 256, 256), BF16), vm(5, 16, 128), vm(16, 128), vm(36, 16, 128),
        vm(12, 16, 128), vm(1024, 128), vm(2, 40, 128),
        vm(1024, 128), vm(1024, 128), vm(1024, 128), vm(1024, 128), field,
        vm(1024, 128), vm(1024, 128), field, vm(1024, 128), field, field, field,
        vm(32, 128), field, vm(9, NCD, ncp), vm(8, 128), vm(8, 8, 128), vm(36, 4, 128), field,
        field, field, field, field, field, field, field, field,
        vm(2, 2, 64, 128), vm(2, 2, 64, 128), vm(2, 4, 4, 128),
        vm(2, 2, 64, 128), vm(2, 2, 64, 128), vm(2, 4, 4, 128),
        vm(6, 2, 16, 128), vm(6, 2, 16, 128), vm(6, 4, 1, 128),
        vm(6, 2, 16, 128), vm(6, 2, 16, 128), vm(6, 4, 1, 128),
        vm(3, nxc, ny, 1, 128), vm(3, nz, 4, 128),
        pltpu.SemaphoreType.DMA((8, 8)), pltpu.SemaphoreType.DMA((8, 8)),
        pltpu.SemaphoreType.DMA((8,)), pltpu.SemaphoreType.DMA((8,)),
        pltpu.SemaphoreType.DMA((8,)), pltpu.SemaphoreType.DMA((8,)),
        pltpu.SemaphoreType.DMA((3, 76)), pltpu.SemaphoreType.DMA((3, 76)),
        pltpu.SemaphoreType.DMA((15,)),
    ]
    anywhere = pl.BlockSpec(memory_space=pl.ANY)
    new, pressure = pl.pallas_call(
        functools.partial(kernel, nx, ny, nxc),
        out_shape=(
            jax.ShapeDtypeStruct((1024, 128), F32),
            jax.ShapeDtypeStruct((256, 128), F32),
        ),
        in_specs=[pl.BlockSpec(memory_space=pltpu.HBM)] * 10,
        out_specs=(anywhere, anywhere),
        scratch_shapes=scratch,
        compiler_params=pltpu.CompilerParams(
            collective_id=0, has_side_effects=True, vmem_limit_bytes=24 << 20
        ),
    )(
        *[pltpu.with_memory_space_constraint(v, pltpu.HBM) for v in (
        fields.reshape(1024, 128),
        viscosity.reshape(256, 128),
        inv_density,
        elem_group,
        coarse,
        cy, bz, cp, spr, fy)],
    )
    new, pressure = pl.pallas_call(
        place,
        out_shape=(
            jax.ShapeDtypeStruct((1024, 128), F32),
            jax.ShapeDtypeStruct((256, 128), F32),
        ),
        in_specs=[anywhere] * 2,
        out_specs=(pl.BlockSpec(memory_space=pltpu.HBM),) * 2,
        scratch_shapes=[pltpu.SemaphoreType.DMA((2,))],
        compiler_params=pltpu.CompilerParams(vmem_limit_bytes=4 << 20),
    )(new, pressure)
    return new.reshape(fields.shape), pressure.reshape(viscosity.shape)


def build(mesh, nxc):
    placed = (
        P(None, "gx", None, "gy", None, None),
        P("gx", None, "gy", None, None),
        P("gx", "gy", None),
        P("gx", "gy", None),
        P(("gx", "gy"), None),
    )
    return jax.shard_map(
        functools.partial(per_device, mesh.shape["gx"], mesh.shape["gy"], nxc),
        mesh=mesh,
        in_specs=placed,
        out_specs=(P(None, "gx", None, "gy", None, None), P("gx", None, "gy", None, None)),
        check_vma=False,
    )


def solution(mesh):
    return build(mesh, XC)
```
